32 devices in a mesh: rep: 2 (over x), seq: 16 (over z, y, core).
Axes of the slice: x: 2, y: 2, z: 4, core: 2. Of those that a mesh axis runs over, the one named last changes fastest.
Arguments:
- q_stream: bfloat16 [4096, 8192], P(('rep', 'seq')), parts along dimension 0, may hold values from -6 to 6
- k_stream: bfloat16 [4096, 8192], P(('rep', 'seq')), parts along dimension 0, may hold values from -6 to 6
- v_stream: bfloat16 [4096, 8192], P(('rep', 'seq')), parts along dimension 0, may hold values from -6 to 6
- feat_filter: float32 [3, 3, 8192], replicated, may hold values from -3.5 to 3.5
- long_filter: bfloat16 [512, 128], replicated, may hold values from -0.5 to 0.5
- skip_gain: float32 [8192], replicated, may hold values from -3 to 3
Outputs:
- mixed: bfloat16 [4096, 8192], P(('rep', 'seq')), parts along dimension 0
The draws below stay inside these ranges and needn't reach their ends.
There are 2 independent parts, one for each index of `rep`. The reference program is written for one: setup_inputs(seed, part) draws one part's arguments, and reference() takes and returns one part's arrays. A program takes and returns all parts, laid end to end along the dimension named above; an argument that names none is the same for every part. Nothing has to cross between parts.
All inputs are finite; a program needn't handle non-finite values.
Results may differ from the reference program's by a relative error of at most 0.005.
Values may be sent and summed in bfloat16 or wider, within the bound.
A program may use at most 128 MiB of HBM per device.

```python
import math
import jax
import jax.numpy as jnp
from jax import lax

D = 8192
GROUP_CH = 16
FILT = 128
FEAT = 3
GROUPS = 512
SEQ_LEN = 2048


def shard_levels(own_key, extent, cuts, least, high):
    loudness = 1.0
    for position, blocks in cuts:
        heights = jax.random.uniform(jax.random.fold_in(jax.random.fold_in(own_key, 6), position), (blocks,), jnp.float32, least / len(cuts), high / len(cuts))
        loudness = loudness * jnp.repeat(jnp.exp(heights), extent[position] // blocks).reshape((-1,) + (1,) * (len(extent) - 1 - position))
    return loudness


def noise(stream_key, shape, scale, limit, cuts=(), kind=jnp.bfloat16):
    level = shard_levels(stream_key, shape, cuts, -0.22, 0.18) if cuts else 1.0
    drawn = jax.random.normal(stream_key, shape, jnp.float32) * scale * level
    return jnp.minimum(jnp.maximum(drawn, -limit), limit).astype(kind)


def setup_inputs(seed: int = 0, part: int = 0) -> dict:
    key_list = jax.random.split(jax.random.key(seed), 7)
    part_keys = jax.random.split(jax.random.fold_in(key_list[6], part), 7)
    return {
        "q_stream": noise(part_keys[0], (SEQ_LEN, D), 1.0, 6.0, ((0, 16),)),
        "k_stream": noise(part_keys[1], (SEQ_LEN, D), 1.0, 6.0, ((0, 16),)),
        "v_stream": noise(part_keys[2], (SEQ_LEN, D), 1.0, 6.0, ((0, 16),)),
        "feat_filter": noise(key_list[3], (3, FEAT, D), FEAT ** -0.5, 3.5, (), jnp.float32),
        "long_filter": noise(key_list[4], (GROUPS, FILT), FILT ** -0.5, 0.5),
        "skip_gain": noise(key_list[5], (D,), 0.5, 3.0, (), jnp.float32),
    }


def featurize(stream, taps):
    length = stream.shape[0]
    padded = jnp.pad(stream.astype(jnp.float32), ((FEAT - 1, 0), (0, 0)))
    total = taps[0] * padded[FEAT - 1:FEAT - 1 + length]
    for j in range(1, FEAT):
        total = total + taps[j] * padded[FEAT - 1 - j:FEAT - 1 - j + length]
    return total


def reference(q_stream, k_stream, v_stream, feat_filter, long_filter, skip_gain):
    length = q_stream.shape[0]
    block = math.gcd(D, 512)
    count = D // block
    expanded = jnp.repeat(long_filter.astype(jnp.float32), GROUP_CH, axis=0).T

    def split(stream):
        return stream.reshape(length, count, block).transpose(1, 0, 2)

    taps_feat = feat_filter.reshape(3, FEAT, count, block).transpose(2, 0, 1, 3)
    taps_long = expanded.reshape(FILT, count, block).transpose(1, 0, 2)
    skips = skip_gain.reshape(count, block)

    def one_block(items):
        query, keys, values, tfeat, tlong, skip = items
        q_feat = featurize(query, tfeat[0])
        k_feat = featurize(keys, tfeat[1])
        v_feat = featurize(values, tfeat[2])
        gated = (k_feat * v_feat).astype(jnp.bfloat16)
        gated_f = gated.astype(jnp.float32)
        padded = jnp.pad(gated_f, ((FILT - 1, 0), (0, 0)))

        def add_tap(j, total):
            return total + tlong[j] * lax.dynamic_slice_in_dim(padded, FILT - 1 - j, length, 0)

        conv = lax.fori_loop(0, FILT, add_tap, jnp.zeros((length, block), jnp.float32))
        return (q_feat * (conv + skip * gated_f)).astype(jnp.bfloat16)

    result = lax.map(one_block, (split(q_stream), split(k_stream), split(v_stream), taps_feat, taps_long, skips))
    return result.transpose(1, 0, 2).reshape(length, D)
```

```python
import functools

import jax
import jax.numpy as jnp
from jax import lax
from jax.experimental import pallas as pl
from jax.experimental.pallas import tpu as pltpu
from jax.sharding import PartitionSpec as P

GROUP_CH = 16
FILT = 128
FEAT = 3
LANES = 128
SUB = 16
CHUNK = 512
EARLY = 4
GRANT = 58 << 20
MESH = pl.DeviceIdType.MESH


def shifted(rim, x):
    ext = jnp.concatenate([rim, x], axis=0)
    return pltpu.roll(ext, 1, 0)[8:], pltpu.roll(ext, 2, 0)[8:]


def featurize(x, rim, taps):
    x = x.astype(jnp.float32)
    one, two = shifted(rim, x)
    return taps[0] * x + taps[1] * one + taps[2] * two


def plan(chunks):
    bounds = [0, EARLY]
    while bounds[-1] < chunks - 1:
        bounds.append(bounds[-1] + max(1, (chunks - bounds[-1]) // 3))
    return list(zip(bounds[:-1], bounds[1:]))


def kernel(
    n, q_hbm, k_hbm, v_hbm, feat_hbm, long_hbm, skip_hbm, mixed,
    q, kv, feat, filt, skip, ends, kv_out, kv_in, q_out, q_in, gated, prev, toep,
    in_sem, end_sem, par_sem, send_sem, recv_sem,
):
    chunks, rows, width = gated.shape
    tiles = width // LANES
    groups = filt.shape[0]
    me = lax.axis_index("seq")
    right, left = lax.rem(me + 1, n), lax.rem(me + n - 1, n)
    has_left, has_right = me > 0, me < n - 1

    barrier = pltpu.get_barrier_semaphore()

    @pl.when(has_left)
    def _():
        pl.semaphore_signal(barrier, inc=1, device_id={"seq": left}, device_id_type=MESH)

    streams = (k_hbm, v_hbm, q_hbm)

    def end_copy(i):
        return pltpu.make_async_copy(
            streams[i].at[pl.ds(rows - 8, 8)], ends.at[i], end_sem.at[i // 2])

    def ends_wait(first, count):
        part = ends.at[pl.ds(first, count)]
        pltpu.make_async_copy(part, part, end_sem.at[first // 2]).wait()

    def cols_of(c):
        return pl.ds(pl.multiple_of(c * width, width), width)

    def kv_load(i, c, group):
        return pltpu.make_async_copy(
            streams[i].at[:, cols_of(c)], kv.at[2 * c + i], in_sem.at[group])

    def kv_wait(first, count, group):
        part = kv.at[pl.ds(2 * first, 2 * count)]
        pltpu.make_async_copy(part, part, in_sem.at[group]).wait()

    def q_load(c):
        return pltpu.make_async_copy(q_hbm.at[:, cols_of(c)], q.at[c], in_sem.at[3])

    params = ((feat_hbm, feat), (long_hbm, filt), (skip_hbm, skip))

    def par_copy(i):
        return pltpu.make_async_copy(params[i][0], params[i][1], par_sem.at[i])

    for i in range(3):
        end_copy(i).start()
    par_copy(0).start()
    kv_load(0, 0, 0).start()
    kv_load(1, 0, 0).start()
    for c in range(1, EARLY):
        kv_load(0, c, 1).start()
        kv_load(1, c, 1).start()

    def remote(src, dst, send, recv):
        return pltpu.make_async_remote_copy(
            src_ref=src, dst_ref=dst, send_sem=send_sem.at[send],
            recv_sem=recv_sem.at[recv], device_id={"seq": right}, device_id_type=MESH)

    def kv_copy():
        return remote(kv_out, kv_in, 1, 0)

    def q_copy():
        return remote(q_out, q_in, 2, 1)

    last = chunks - 1
    groups_of = plan(chunks)

    def piece(c, group, part=slice(None), lanes=slice(None)):
        return remote(gated.at[c, part, lanes], prev.at[c, part, lanes], 0, 2 + group)

    def arrived(first, count, group):
        part = prev.at[pl.ds(first, count)]
        pltpu.make_async_copy(part, part, recv_sem.at[2 + group]).wait()

    HEAD, BODY = pl.ds(0, 16), pl.ds(16, rows - 16)

    def last_copy(t):
        return piece(last, len(groups_of) + t, pl.ds(0, rows), pl.ds(t * LANES, LANES))

    row = lax.broadcasted_iota(jnp.int32, (8, LANES), 0)

    def last_rows(i, at):
        return ends[i, :, pl.ds(pl.multiple_of(at, LANES), LANES)].astype(jnp.float32)

    def pack_kv():
        half = kv_out.shape[1]

        @pl.loop(0, half // width)
        def _(c):
            for t in range(tiles):
                at = c * width + t * LANES
                packed = jnp.where(
                    row < 2, pltpu.roll(last_rows(0, at), 2, 0),
                    jnp.where(
                        row < 4, pltpu.roll(last_rows(1, at), 4, 0),
                        jnp.where(
                            row < 6, pltpu.roll(last_rows(0, at + half), 6, 0),
                            last_rows(1, at + half))))
                kv_out[:, pl.ds(pl.multiple_of(at, LANES), LANES)] = packed.astype(jnp.bfloat16)

    def pack_q():
        fourth = q_out.shape[1]

        @pl.loop(0, fourth // width)
        def _(c):
            for t in range(tiles):
                at = c * width + t * LANES
                packed = last_rows(2, at + 3 * fourth)
                for m in range(3):
                    packed = jnp.where(
                        row // 2 == m, pltpu.roll(last_rows(2, at + m * fourth), 2 + 2 * m, 0),
                        packed)
                q_out[:, pl.ds(pl.multiple_of(at, LANES), LANES)] = packed.astype(jnp.bfloat16)

    def taps_of(i, cols):
        return [feat[i, pl.ds(j, 1), cols] for j in range(FEAT)]

    def kv_rims(c, t):
        per_half = chunks // 2
        upper = c >= per_half
        at = lax.rem(c, per_half) * width + t * LANES
        x = kv_in[:, pl.ds(pl.multiple_of(at, LANES), LANES)].astype(jnp.float32)
        return (jnp.where(upper, pltpu.roll(x, 2, 0), pltpu.roll(x, 6, 0)),
                jnp.where(upper, x, pltpu.roll(x, 4, 0)))

    def q_rim(c, t):
        per_fourth = chunks // 4
        m = c // per_fourth
        at = lax.rem(c, per_fourth) * width + t * LANES
        x = q_in[:, pl.ds(pl.multiple_of(at, LANES), LANES)].astype(jnp.float32)
        rim = x
        for i in range(3):
            rim = jnp.where(m == i, pltpu.roll(x, 6 - 2 * i, 0), rim)
        return rim

    def columns(c, t):
        return pl.ds(pl.multiple_of(c * width + t * LANES, LANES), LANES)

    def gate(c, t, first, count, k_rim, v_rim):
        cols = columns(c, t)
        part, lanes = pl.ds(first, count), pl.ds(t * LANES, LANES)
        k_feat = featurize(kv[2 * c, part, lanes], k_rim, taps_of(1, cols))
        v_feat = featurize(kv[2 * c + 1, part, lanes], v_rim, taps_of(2, cols))
        return (k_feat * v_feat).astype(jnp.bfloat16)

    ends_wait(0, 2)
    pack_kv()

    @pl.when(has_right)
    def _():
        pl.semaphore_wait(barrier, 1)
        kv_copy().start()

    ends_wait(2, 1)
    pack_q()

    @pl.when(has_right)
    def _():
        q_copy().start()

    zeros = jnp.zeros((8, LANES), jnp.float32)
    par_copy(0).wait()
    for c in range(EARLY):
        if c == 0:
            kv_wait(0, 1, 0)
        elif c == 1:
            kv_wait(1, EARLY - 1, 1)
        for t in range(tiles):
            lanes = pl.ds(t * LANES, LANES)
            gated[c, BODY, lanes] = gate(c, t, 0, rows, zeros, zeros)[16:]
            if c == 0 and t % 2 == 1:
                @pl.when(has_right)
                def _():
                    piece(0, 0, BODY, pl.ds((t - 1) * LANES, 2 * LANES)).start()

        if c > 0:
            @pl.when(has_right)
            def _():
                piece(c, 0, BODY).start()

    @pl.loop(EARLY, chunks)
    def _(c):
        kv_load(0, c, 2).start()
        kv_load(1, c, 2).start()

    @pl.when(has_left)
    def _():
        kv_copy().wait_recv()

    @pl.when(jnp.logical_not(has_left))
    def _():
        kv_in[...] = jnp.zeros_like(kv_in)
        q_in[...] = jnp.zeros_like(q_in)

        @pl.loop(0, chunks)
        def _(c):
            prev[c] = jnp.zeros((rows, width), jnp.bfloat16)

    for c in range(EARLY):
        for t in range(tiles):
            gated[c, pl.ds(0, 16), pl.ds(t * LANES, LANES)] = gate(
                c, t, 0, 16, *kv_rims(c, t))

        @pl.when(has_right)
        def _():
            piece(c, 0, HEAD).start()

    par_copy(1).start()
    par_copy(2).start()

    @pl.loop(0, chunks)
    def _(c):
        q_load(c).start()

    kv_wait(EARLY, chunks - EARLY, 2)
    for g, (first, stop) in enumerate(groups_of):
        if g == 0:
            continue

        @pl.loop(first, stop)
        def _(c):
            for t in range(tiles):
                gated[c, :, pl.ds(t * LANES, LANES)] = gate(c, t, 0, rows, *kv_rims(c, t))

            @pl.when(has_right)
            def _():
                piece(c, g).start()

    for t in range(tiles):
        gated[last, :, pl.ds(t * LANES, LANES)] = gate(last, t, 0, rows, *kv_rims(last, t))

        @pl.when(has_right)
        def _():
            last_copy(t).start()

    par_copy(1).wait()
    par_copy(2).wait()
    taps = lax.broadcasted_iota(jnp.int32, (FILT, 2 * LANES), 0)
    place = lax.broadcasted_iota(jnp.int32, (FILT, 2 * LANES), 1)
    total = taps + place
    for b in range(SUB):
        onehot = jnp.where(total == FILT + b, 1.0, 0.0).astype(jnp.bfloat16)
        moved = jnp.dot(filt[...], onehot, preferred_element_type=jnp.float32)
        for r in range(2):
            toep[r, pl.ds(b, groups, stride=SUB), :] = moved[:, r * LANES:(r + 1) * LANES]

    lane_group = lax.broadcasted_iota(jnp.int32, (SUB, LANES), 1) // GROUP_CH
    per_tile = LANES // GROUP_CH
    blocks = rows // SUB
    depth = FILT + SUB

    def mix(c, only=None):
        for t in range(tiles) if only is None else (only,):
            cols, lanes = columns(c, t), pl.ds(t * LANES, LANES)
            first = pl.multiple_of((c * tiles + t) * LANES, LANES)
            own = gated[c, :, lanes]
            window = jnp.concatenate([prev[c, :, lanes], own], axis=0)
            left_part = toep[0, pl.ds(first, LANES), :].astype(jnp.bfloat16)
            right_part = toep[1, pl.ds(first, LANES), :].astype(jnp.bfloat16)
            lhs = jnp.concatenate([left_part, right_part[:, :depth - LANES]], axis=1)
            rhs = jnp.concatenate(
                [window[a * SUB:a * SUB + depth] for a in range(blocks)], axis=1)
            every = jnp.dot(lhs, rhs, preferred_element_type=jnp.float32)
            conv = []
            for a in range(blocks):
                mine = every[:SUB, a * LANES:(a + 1) * LANES]
                for g in range(1, per_tile):
                    mine = jnp.where(
                        lane_group == g,
                        every[g * SUB:(g + 1) * SUB, a * LANES:(a + 1) * LANES], mine)
                conv.append(mine)
            conv = jnp.concatenate(conv, axis=0)
            q_feat = featurize(q[c, :, lanes], q_rim(c, t), taps_of(0, cols))
            direct = skip[:, cols] * own.astype(jnp.float32)
            mixed[c, :, lanes] = (q_feat * (conv + direct)).astype(jnp.bfloat16)

    @pl.when(has_left)
    def _():
        q_copy().wait_recv()

    pltpu.make_async_copy(q, q, in_sem.at[3]).wait()
    for g, (first, stop) in enumerate(groups_of):
        @pl.when(has_left)
        def _():
            arrived(first, stop - first, g)

        @pl.loop(first, stop)
        def _(c):
            mix(c)

    for t in range(tiles):
        @pl.when(has_left)
        def _():
            last_copy(t).wait_recv()

        mix(last, t)

    @pl.when(has_right)
    def _():
        kv_copy().wait_send()
        q_copy().wait_send()
        pltpu.make_async_copy(gated, gated, send_sem.at[0]).wait()


def drain(mixed, out_hbm, sem):
    chunks, _, width = mixed.shape

    for c in range(chunks):
        pltpu.make_async_copy(
            mixed.at[c], out_hbm.at[:, c * width:(c + 1) * width], sem.at[0]).start()
    pltpu.make_async_copy(mixed, mixed, sem.at[0]).wait()


def shards(n, q_stream, k_stream, v_stream, feat_filter, long_filter, skip_gain):
    rows, channels = q_stream.shape
    groups = long_filter.shape[0]
    chunks = channels // CHUNK
    cut = pltpu.VMEM((chunks, rows, CHUNK), jnp.bfloat16)
    dma = pltpu.SemaphoreType.DMA
    arrivals = 2 + len(plan(chunks)) + CHUNK // LANES
    mixed = pl.pallas_call(
        functools.partial(kernel, n),
        out_shape=cut,
        in_specs=[pl.BlockSpec(memory_space=pltpu.HBM)] * 6,
        out_specs=pl.BlockSpec(memory_space=pltpu.VMEM),
        scratch_shapes=[
            cut, pltpu.VMEM((2 * chunks, rows, CHUNK), jnp.bfloat16),
            pltpu.VMEM(feat_filter.shape, jnp.float32),
            pltpu.VMEM(long_filter.shape, jnp.bfloat16),
            pltpu.VMEM((1, channels), jnp.float32),
            pltpu.VMEM((3, 8, channels), jnp.bfloat16),
            pltpu.VMEM((8, channels // 2), jnp.bfloat16),
            pltpu.VMEM((8, channels // 2), jnp.bfloat16),
            pltpu.VMEM((8, channels // 4), jnp.bfloat16),
            pltpu.VMEM((8, channels // 4), jnp.bfloat16),
            cut, cut,
            pltpu.VMEM((2, groups * SUB, LANES), jnp.float32),
            dma((4,)), dma((2,)), dma((3,)), dma((3,)), dma((arrivals,)),
        ],
        compiler_params=pltpu.CompilerParams(
            collective_id=0, has_side_effects=True, vmem_limit_bytes=GRANT),
    )(q_stream, k_stream, v_stream, feat_filter, long_filter, skip_gain.reshape(1, channels))
    return pl.pallas_call(
        drain,
        out_shape=jax.ShapeDtypeStruct((rows, channels), jnp.bfloat16),
        in_specs=[pl.BlockSpec(memory_space=pltpu.VMEM)],
        out_specs=pl.BlockSpec(memory_space=pl.ANY),
        scratch_shapes=[dma((1,))],
        compiler_params=pltpu.CompilerParams(vmem_limit_bytes=8 << 20),
    )(mixed)


def solution(mesh):
    n = mesh.shape["seq"]
    rows = P(("rep", "seq"), None)
    return jax.shard_map(
        functools.partial(shards, n), mesh=mesh,
        in_specs=(rows, rows, rows, P(), P(), P()), out_specs=rows, check_vma=False)
```

```python
import functools

import jax
import jax.numpy as jnp
from jax import lax
from jax.experimental import pallas as pl
from jax.experimental.pallas import tpu as pltpu
from jax.sharding import PartitionSpec as P

GROUP_CH = 16
FILT = 128
FEAT = 3
LANES = 128
SUB = 16
CHUNK = 512
EARLY = 4
HOPS = 3
AIDE = 0
GRANT = 58 << 20
MESH = pl.DeviceIdType.MESH


def shifted(rim, x):
    ext = jnp.concatenate([rim, x], axis=0)
    return pltpu.roll(ext, 1, 0)[8:], pltpu.roll(ext, 2, 0)[8:]


def featurize(x, rim, taps):
    x = x.astype(jnp.float32)
    one, two = shifted(rim, x)
    return taps[0] * x + taps[1] * one + taps[2] * two


def row_of(mesh):
    ring = mesh.devices.reshape(-1, mesh.shape["seq"])[0]
    at = [getattr(d, "coords", None) for d in ring]
    if None in at:
        return 0
    apart = [sum(p != q for p, q in zip(a, b)) for a, b in zip(at, at[1:])]
    turns = [i + 1 for i, axes in enumerate(apart) if axes > 1]
    row = turns[0] if turns else 0
    return row if row > 2 and len(ring) % row == 0 else 0


def kernel(
    n, line, q_hbm, k_hbm, v_hbm, feat_hbm, long_hbm, skip_hbm, mixed,
    q, kv, feat, filt, skip, ends, kv_out, kv_in, q_out, q_in, gated, prev, toep,
    hop, in_sem, end_sem, par_sem, send_sem, recv_sem, hop_sem,
):
    chunks, rows, width = gated.shape
    tiles = width // LANES
    groups = filt.shape[0]
    me = lax.axis_index("seq")
    right, left = lax.rem(me + 1, n), lax.rem(me + n - 1, n)
    has_left, has_right = me > 0, me < n - 1

    barrier = pltpu.get_barrier_semaphore()

    @pl.when(has_left)
    def _():
        pl.semaphore_signal(barrier, inc=1, device_id={"seq": left}, device_id_type=MESH)

    hops = hop_sem.shape[0] if line else 0
    if line:
        spot, level = lax.rem(me, line), me // line
        behind = n // line - 1 - level
        turns = jnp.logical_and(spot == line - 1, has_right)
        carries = jnp.logical_and(spot == AIDE, behind > 0)
        plain = jnp.logical_and(has_right, jnp.logical_not(turns))

        @pl.when(carries)
        def _():
            pl.semaphore_signal(
                barrier, inc=1, device_id={"seq": me + line - 1 - AIDE}, device_id_type=MESH)

    else:
        plain = has_right

    streams = (k_hbm, v_hbm, q_hbm)

    def end_copy(i):
        return pltpu.make_async_copy(
            streams[i].at[pl.ds(rows - 8, 8)], ends.at[i], end_sem.at[i // 2])

    def ends_wait(first, count):
        part = ends.at[pl.ds(first, count)]
        pltpu.make_async_copy(part, part, end_sem.at[first // 2]).wait()

    def cols_of(c):
        return pl.ds(pl.multiple_of(c * width, width), width)

    def kv_load(i, c, group):
        return pltpu.make_async_copy(
            streams[i].at[:, cols_of(c)], kv.at[2 * c + i], in_sem.at[group])

    def kv_wait(first, count, group):
        part = kv.at[pl.ds(2 * first, 2 * count)]
        pltpu.make_async_copy(part, part, in_sem.at[group]).wait()

    def q_load(c):
        return pltpu.make_async_copy(q_hbm.at[:, cols_of(c)], q.at[c], in_sem.at[3])

    params = ((feat_hbm, feat), (long_hbm, filt), (skip_hbm, skip))

    def par_copy(i):
        return pltpu.make_async_copy(params[i][0], params[i][1], par_sem.at[i])

    for i in range(3):
        end_copy(i).start()
    par_copy(0).start()
    kv_load(0, 0, 0).start()
    kv_load(1, 0, 0).start()
    for c in range(1, EARLY):
        kv_load(0, c, 1).start()
        kv_load(1, c, 1).start()

    def remote(src, dst, send, recv, to=right):
        return pltpu.make_async_remote_copy(
            src_ref=src, dst_ref=dst, send_sem=send_sem.at[send], recv_sem=recv,
            device_id={"seq": to}, device_id_type=MESH)

    def kv_copy():
        return remote(kv_out, kv_in, 1, recv_sem.at[0])

    def q_copy():
        return remote(q_out, q_in, 2, recv_sem.at[1])

    last = chunks - 1
    pairs = last // 2
    def piece(c, group, part=slice(None), lanes=slice(None), send=0):
        return remote(
            gated.at[c, part, lanes], prev.at[c, part, lanes], send, recv_sem.at[2 + group])

    def sent(part, slot):
        pltpu.make_async_copy(part, part, send_sem.at[slot]).wait()

    def arrived(first, count, group):
        part = prev.at[pl.ds(first, count)]
        pltpu.make_async_copy(part, part, recv_sem.at[2 + group]).wait()

    HEAD, BODY = pl.ds(0, 16), pl.ds(16, rows - 16)

    def hop_copy(h):
        return remote(
            gated.at[h, BODY], hop.at[h, BODY], 6 + h, hop_sem.at[h],
            jnp.maximum(me - line + 1 + AIDE, 0))

    def forward_copy(h):
        return remote(
            hop.at[h, BODY], prev.at[h, BODY], 3, recv_sem.at[2 + h // 2],
            jnp.minimum(me + line - AIDE, n - 1))

    def carry(h):
        @pl.when(jnp.logical_and(carries, h < behind))
        def _():
            hop_copy(h).wait_recv()
            forward_copy(h).start()

    def last_copy(t):
        return piece(last, pairs + 1 + t, pl.ds(0, rows), pl.ds(t * LANES, LANES))

    row = lax.broadcasted_iota(jnp.int32, (8, LANES), 0)

    def last_rows(i, at):
        return ends[i, :, pl.ds(pl.multiple_of(at, LANES), LANES)].astype(jnp.float32)

    def pack_kv():
        half = kv_out.shape[1]

        @pl.loop(0, half // width)
        def _(c):
            for t in range(tiles):
                at = c * width + t * LANES
                packed = jnp.where(
                    row < 2, pltpu.roll(last_rows(0, at), 2, 0),
                    jnp.where(
                        row < 4, pltpu.roll(last_rows(1, at), 4, 0),
                        jnp.where(
                            row < 6, pltpu.roll(last_rows(0, at + half), 6, 0),
                            last_rows(1, at + half))))
                kv_out[:, pl.ds(pl.multiple_of(at, LANES), LANES)] = packed.astype(jnp.bfloat16)

    def pack_q():
        fourth = q_out.shape[1]

        @pl.loop(0, fourth // width)
        def _(c):
            for t in range(tiles):
                at = c * width + t * LANES
                packed = last_rows(2, at + 3 * fourth)
                for m in range(3):
                    packed = jnp.where(
                        row // 2 == m, pltpu.roll(last_rows(2, at + m * fourth), 2 + 2 * m, 0),
                        packed)
                q_out[:, pl.ds(pl.multiple_of(at, LANES), LANES)] = packed.astype(jnp.bfloat16)

    def taps_of(i, cols):
        return [feat[i, pl.ds(j, 1), cols] for j in range(FEAT)]

    def kv_rims(c, t):
        per_half = chunks // 2
        upper = c >= per_half
        at = lax.rem(c, per_half) * width + t * LANES
        x = kv_in[:, pl.ds(pl.multiple_of(at, LANES), LANES)].astype(jnp.float32)
        return (jnp.where(upper, pltpu.roll(x, 2, 0), pltpu.roll(x, 6, 0)),
                jnp.where(upper, x, pltpu.roll(x, 4, 0)))

    def q_rim(c, t):
        per_fourth = chunks // 4
        m = c // per_fourth
        at = lax.rem(c, per_fourth) * width + t * LANES
        x = q_in[:, pl.ds(pl.multiple_of(at, LANES), LANES)].astype(jnp.float32)
        rim = x
        for i in range(3):
            rim = jnp.where(m == i, pltpu.roll(x, 6 - 2 * i, 0), rim)
        return rim

    def columns(c, t):
        return pl.ds(pl.multiple_of(c * width + t * LANES, LANES), LANES)

    def gate(c, t, first, count, k_rim, v_rim):
        cols = columns(c, t)
        part, lanes = pl.ds(first, count), pl.ds(t * LANES, LANES)
        k_feat = featurize(kv[2 * c, part, lanes], k_rim, taps_of(1, cols))
        v_feat = featurize(kv[2 * c + 1, part, lanes], v_rim, taps_of(2, cols))
        return (k_feat * v_feat).astype(jnp.bfloat16)

    ends_wait(0, 2)
    pack_kv()

    if line:
        @pl.when(turns)
        def _():
            pl.semaphore_wait(barrier, 2)

        @pl.when(jnp.logical_and(has_right, jnp.logical_not(turns)))
        def _():
            pl.semaphore_wait(barrier, 1)
    else:
        @pl.when(has_right)
        def _():
            pl.semaphore_wait(barrier, 1)

    @pl.when(has_right)
    def _():
        kv_copy().start()

    ends_wait(2, 1)
    pack_q()

    @pl.when(has_right)
    def _():
        q_copy().start()

    zeros = jnp.zeros((8, LANES), jnp.float32)
    par_copy(0).wait()
    for c in range(EARLY):
        if c == 0:
            kv_wait(0, 1, 0)
        elif c == 1:
            kv_wait(1, EARLY - 1, 1)
        for t in range(tiles):
            lanes = pl.ds(t * LANES, LANES)
            gated[c, BODY, lanes] = gate(c, t, 0, rows, zeros, zeros)[16:]
            if c == 0 and t % 2 == 1:
                @pl.when(plain)
                def _():
                    piece(0, 0, BODY, pl.ds((t - 1) * LANES, 2 * LANES), 4).start()

        if hops:
            if c < hops:
                @pl.when(jnp.logical_and(turns, c < behind))
                def _():
                    hop_copy(c).start()

            if 0 < c <= hops:
                @pl.when(jnp.logical_and(turns, behind == c))
                def _():
                    for h in range(c - 1):
                        hop_copy(h).wait_send()

            if c == hops:
                @pl.when(jnp.logical_and(turns, behind > c))
                def _():
                    for h in range(c):
                        hop_copy(h).wait_send()

            if c > 0:
                @pl.when(jnp.logical_and(turns, c >= jnp.minimum(behind, hops)))
                def _():
                    piece(c, c // 2, BODY, send=4).start()

        if c > 0:
            @pl.when(plain)
            def _():
                piece(c, c // 2, BODY, send=4).start()

    @pl.loop(EARLY, chunks)
    def _(c):
        kv_load(0, c, 2).start()
        kv_load(1, c, 2).start()

    @pl.when(has_left)
    def _():
        kv_copy().wait_recv()

    @pl.when(jnp.logical_not(has_left))
    def _():
        kv_in[...] = jnp.zeros_like(kv_in)
        q_in[...] = jnp.zeros_like(q_in)

        @pl.loop(0, chunks)
        def _(c):
            prev[c] = jnp.zeros((rows, width), jnp.bfloat16)

    for c in range(EARLY):
        for t in range(tiles):
            gated[c, pl.ds(0, 16), pl.ds(t * LANES, LANES)] = gate(
                c, t, 0, 16, *kv_rims(c, t))

        @pl.when(has_right)
        def _():
            piece(c, c // 2, HEAD, send=5).start()

    par_copy(1).start()
    par_copy(2).start()

    @pl.loop(0, chunks)
    def _(c):
        q_load(c).start()

    kv_wait(EARLY, chunks - EARLY, 2)
    @pl.loop(EARLY, last)
    def _(c):
        for t in range(tiles):
            gated[c, :, pl.ds(t * LANES, LANES)] = gate(c, t, 0, rows, *kv_rims(c, t))

        @pl.when(has_right)
        def _():
            piece(c, c // 2).start()

    for t in range(tiles):
        gated[last, :, pl.ds(t * LANES, LANES)] = gate(last, t, 0, rows, *kv_rims(last, t))

        @pl.when(has_right)
        def _():
            last_copy(t).start()

    par_copy(1).wait()
    par_copy(2).wait()
    taps = lax.broadcasted_iota(jnp.int32, (FILT, 2 * LANES), 0)
    place = lax.broadcasted_iota(jnp.int32, (FILT, 2 * LANES), 1)
    total = taps + place
    for b in range(SUB):
        onehot = jnp.where(total == FILT + b, 1.0, 0.0).astype(jnp.bfloat16)
        moved = jnp.dot(filt[...], onehot, preferred_element_type=jnp.float32)
        for r in range(2):
            toep[r, pl.ds(b, groups, stride=SUB), :] = moved[:, r * LANES:(r + 1) * LANES]

    lane_group = lax.broadcasted_iota(jnp.int32, (SUB, LANES), 1) // GROUP_CH
    per_tile = LANES // GROUP_CH
    blocks = rows // SUB
    depth = FILT + SUB

    def mix(c, only=None):
        for t in range(tiles) if only is None else (only,):
            cols, lanes = columns(c, t), pl.ds(t * LANES, LANES)
            first = pl.multiple_of((c * tiles + t) * LANES, LANES)
            own = gated[c, :, lanes]
            window = jnp.concatenate([prev[c, :, lanes], own], axis=0)
            left_part = toep[0, pl.ds(first, LANES), :].astype(jnp.bfloat16)
            right_part = toep[1, pl.ds(first, LANES), :].astype(jnp.bfloat16)
            lhs = jnp.concatenate([left_part, right_part[:, :depth - LANES]], axis=1)
            rhs = jnp.concatenate(
                [window[a * SUB:a * SUB + depth] for a in range(blocks)], axis=1)
            every = jnp.dot(lhs, rhs, preferred_element_type=jnp.float32)
            conv = []
            for a in range(blocks):
                mine = every[:SUB, a * LANES:(a + 1) * LANES]
                for g in range(1, per_tile):
                    mine = jnp.where(
                        lane_group == g,
                        every[g * SUB:(g + 1) * SUB, a * LANES:(a + 1) * LANES], mine)
                conv.append(mine)
            conv = jnp.concatenate(conv, axis=0)
            q_feat = featurize(q[c, :, lanes], q_rim(c, t), taps_of(0, cols))
            direct = skip[:, cols] * own.astype(jnp.float32)
            mixed[c, :, lanes] = (q_feat * (conv + direct)).astype(jnp.bfloat16)

    @pl.when(has_left)
    def _():
        q_copy().wait_recv()

    pltpu.make_async_copy(q, q, in_sem.at[3]).wait()
    for h in range(hops):
        carry(h)

    @pl.loop(0, pairs)
    def _(i):
        @pl.when(has_left)
        def _():
            arrived(2 * i, 2, i)

        @pl.loop(2 * i, 2 * i + 2)
        def _(c):
            mix(c)

    for c in range(2 * pairs, last):
        @pl.when(has_left)
        def _():
            arrived(c, 1, pairs)

        mix(c)

    for t in range(tiles):
        @pl.when(has_left)
        def _():
            last_copy(t).wait_recv()

        mix(last, t)

    @pl.when(has_right)
    def _():
        kv_copy().wait_send()
        q_copy().wait_send()
        sent(gated.at[pl.ds(EARLY, chunks - EARLY)], 0)
        sent(gated.at[pl.ds(0, EARLY), HEAD], 5)

    @pl.when(plain)
    def _():
        sent(gated.at[pl.ds(0, EARLY), BODY], 4)

    if hops:
        for b in range(1, hops + 1):
            held = behind == b if b < hops else behind >= b

            @pl.when(jnp.logical_and(turns, held))
            def _():
                sent(gated.at[pl.ds(0, EARLY - b), BODY], 4)

            @pl.when(jnp.logical_and(carries, held))
            def _():
                sent(hop.at[pl.ds(0, b), BODY], 3)

            @pl.when(jnp.logical_and(turns, behind == b))
            def _():
                hop_copy(b - 1).wait_send()


def drain(mixed, out_hbm, sem):
    chunks, _, width = mixed.shape

    for c in range(chunks):
        pltpu.make_async_copy(
            mixed.at[c], out_hbm.at[:, c * width:(c + 1) * width], sem.at[0]).start()
    pltpu.make_async_copy(mixed, mixed, sem.at[0]).wait()


def shards(n, line, q_stream, k_stream, v_stream, feat_filter, long_filter, skip_gain):
    rows, channels = q_stream.shape
    groups = long_filter.shape[0]
    chunks = channels // CHUNK
    cut = pltpu.VMEM((chunks, rows, CHUNK), jnp.bfloat16)
    dma = pltpu.SemaphoreType.DMA
    hops = HOPS if line else 0
    arrivals = 3 + (chunks - 1) // 2 + CHUNK // LANES
    hops = max(hops, 1)
    mixed = pl.pallas_call(
        functools.partial(kernel, n, line),
        out_shape=cut,
        in_specs=[pl.BlockSpec(memory_space=pltpu.HBM)] * 6,
        out_specs=pl.BlockSpec(memory_space=pltpu.VMEM),
        scratch_shapes=[
            cut, pltpu.VMEM((2 * chunks, rows, CHUNK), jnp.bfloat16),
            pltpu.VMEM(feat_filter.shape, jnp.float32),
            pltpu.VMEM(long_filter.shape, jnp.bfloat16),
            pltpu.VMEM((1, channels), jnp.float32),
            pltpu.VMEM((3, 8, channels), jnp.bfloat16),
            pltpu.VMEM((8, channels // 2), jnp.bfloat16),
            pltpu.VMEM((8, channels // 2), jnp.bfloat16),
            pltpu.VMEM((8, channels // 4), jnp.bfloat16),
            pltpu.VMEM((8, channels // 4), jnp.bfloat16),
            cut, cut,
            pltpu.VMEM((2, groups * SUB, LANES), jnp.float32),
            pltpu.VMEM((hops, rows, CHUNK), jnp.bfloat16),
            dma((4,)), dma((2,)), dma((3,)), dma((6 + (hops if line else 0),)), dma((arrivals,)), dma((hops,)),
        ],
        compiler_params=pltpu.CompilerParams(
            collective_id=0, has_side_effects=True, vmem_limit_bytes=GRANT),
    )(q_stream, k_stream, v_stream, feat_filter, long_filter, skip_gain.reshape(1, channels))
    return pl.pallas_call(
        drain,
        out_shape=jax.ShapeDtypeStruct((rows, channels), jnp.bfloat16),
        in_specs=[pl.BlockSpec(memory_space=pltpu.VMEM)],
        out_specs=pl.BlockSpec(memory_space=pl.ANY),
        scratch_shapes=[dma((1,))],
        compiler_params=pltpu.CompilerParams(vmem_limit_bytes=8 << 20),
    )(mixed)


def solution(mesh):
    n = mesh.shape["seq"]
    rows = P(("rep", "seq"), None)
    return jax.shard_map(
        functools.partial(shards, n, row_of(mesh)), mesh=mesh,
        in_specs=(rows, rows, rows, P(), P(), P()), out_specs=rows, check_vma=False)
```

```python
import functools

import jax
import jax.numpy as jnp
from jax import lax
from jax.experimental import pallas as pl
from jax.experimental.pallas import tpu as pltpu
from jax.sharding import PartitionSpec as P

GROUP_CH = 16
FILT = 128
FEAT = 3
LANES = 128
SUB = 16
CHUNK = 512
EARLY = 4
HOPS = 3
AIDE = 0
GRANT = 59 << 20
MESH = pl.DeviceIdType.MESH


def shifted(rim, x):
    ext = jnp.concatenate([rim, x], axis=0)
    return pltpu.roll(ext, 1, 0)[8:], pltpu.roll(ext, 2, 0)[8:]


def featurize(x, rim, taps):
    x = x.astype(jnp.float32)
    one, two = shifted(rim, x)
    return taps[0] * x + taps[1] * one + taps[2] * two


def row_of(mesh):
    ring = mesh.devices.reshape(-1, mesh.shape["seq"])[0]
    at = [getattr(d, "coords", None) for d in ring]
    if None in at:
        return 0
    apart = [sum(p != q for p, q in zip(a, b)) for a, b in zip(at, at[1:])]
    turns = [i + 1 for i, axes in enumerate(apart) if axes > 1]
    row = turns[0] if turns else 0
    return row if row > 2 and len(ring) % row == 0 else 0


def convolve(lhs, window):
    rows = window.shape[0] - FILT
    blocks = rows // SUB
    depth = FILT + SUB
    lane_group = lax.broadcasted_iota(jnp.int32, (SUB, LANES), 1) // GROUP_CH
    rhs = jnp.concatenate([window[a * SUB:a * SUB + depth] for a in range(blocks)], axis=1)
    every = jnp.dot(lhs, rhs, preferred_element_type=jnp.float32)
    conv = []
    for a in range(blocks):
        mine = every[:SUB, a * LANES:(a + 1) * LANES]
        for g in range(1, LANES // GROUP_CH):
            mine = jnp.where(
                lane_group == g,
                every[g * SUB:(g + 1) * SUB, a * LANES:(a + 1) * LANES], mine)
        conv.append(mine)
    return jnp.concatenate(conv, axis=0)


def kernel(
    n, line, q_hbm, k_hbm, v_hbm, feat_hbm, long_hbm, skip_hbm,
    mixed, end_window, end_lhs, end_q, end_direct,
    q, kv, feat, filt, skip, ends, kv_out, kv_in, q_out, q_in, gated, prev, toep,
    hop, in_sem, end_sem, par_sem, send_sem, recv_sem, hop_sem,
):
    chunks, rows, width = gated.shape
    tiles = width // LANES
    groups = filt.shape[0]
    me = lax.axis_index("seq")
    right, left = lax.rem(me + 1, n), lax.rem(me + n - 1, n)
    has_left, has_right = me > 0, me < n - 1

    barrier = pltpu.get_barrier_semaphore()

    @pl.when(has_left)
    def _():
        pl.semaphore_signal(barrier, inc=1, device_id={"seq": left}, device_id_type=MESH)

    hops = hop_sem.shape[0] if line else 0
    if line:
        spot, level = lax.rem(me, line), me // line
        behind = n // line - 1 - level
        turns = jnp.logical_and(spot == line - 1, has_right)
        carries = jnp.logical_and(spot == AIDE, behind > 0)
        plain = jnp.logical_and(has_right, jnp.logical_not(turns))

        @pl.when(carries)
        def _():
            pl.semaphore_signal(
                barrier, inc=1, device_id={"seq": me + line - 1 - AIDE}, device_id_type=MESH)

    else:
        plain = has_right

    streams = (k_hbm, v_hbm, q_hbm)

    def end_copy(i):
        return pltpu.make_async_copy(
            streams[i].at[pl.ds(rows - 8, 8)], ends.at[i], end_sem.at[i // 2])

    def ends_wait(first, count):
        part = ends.at[pl.ds(first, count)]
        pltpu.make_async_copy(part, part, end_sem.at[first // 2]).wait()

    def cols_of(c):
        return pl.ds(pl.multiple_of(c * width, width), width)

    def kv_load(i, c, group):
        return pltpu.make_async_copy(
            streams[i].at[:, cols_of(c)], kv.at[2 * c + i], in_sem.at[group])

    def kv_wait(first, count, group):
        part = kv.at[pl.ds(2 * first, 2 * count)]
        pltpu.make_async_copy(part, part, in_sem.at[group]).wait()

    def q_load(c):
        return pltpu.make_async_copy(q_hbm.at[:, cols_of(c)], q.at[c], in_sem.at[0])

    params = (
        (feat_hbm, feat, par_sem.at[0]), (long_hbm, filt, end_sem.at[0]),
        (skip_hbm, skip, end_sem.at[1]))

    def par_copy(i):
        return pltpu.make_async_copy(*params[i])

    for i in range(3):
        end_copy(i).start()
    par_copy(0).start()
    kv_load(0, 0, 0).start()
    kv_load(1, 0, 0).start()
    for c in range(1, EARLY):
        kv_load(0, c, 1).start()
        kv_load(1, c, 1).start()

    def remote(src, dst, send, recv, to=right):
        return pltpu.make_async_remote_copy(
            src_ref=src, dst_ref=dst, send_sem=send_sem.at[send], recv_sem=recv,
            device_id={"seq": to}, device_id_type=MESH)

    def kv_copy():
        return remote(kv_out, kv_in, 1, recv_sem.at[0])

    def q_copy():
        return remote(q_out, q_in, 2, recv_sem.at[1])

    last = chunks - 1
    pairs = last // 2
    def piece(c, group, part=slice(None), lanes=slice(None), send=0):
        return remote(
            gated.at[c, part, lanes], prev.at[c, part, lanes], send, recv_sem.at[2 + group])

    def sent(part, slot):
        pltpu.make_async_copy(part, part, send_sem.at[slot]).wait()

    def arrived(first, count, group):
        part = prev.at[pl.ds(first, count)]
        pltpu.make_async_copy(part, part, recv_sem.at[2 + group]).wait()

    HEAD, BODY = pl.ds(0, 16), pl.ds(16, rows - 16)

    def hop_copy(h):
        return remote(
            gated.at[h, BODY], hop.at[h, BODY], 5 + h, hop_sem.at[h],
            jnp.maximum(me - line + 1 + AIDE, 0))

    def forward_copy(h):
        return remote(
            hop.at[h, BODY], prev.at[h, BODY], 5, recv_sem.at[2 + h // 2],
            jnp.minimum(me + line - AIDE, n - 1))

    def carry(h):
        @pl.when(jnp.logical_and(carries, h < behind))
        def _():
            hop_copy(h).wait_recv()
            forward_copy(h).start()

    row = lax.broadcasted_iota(jnp.int32, (8, LANES), 0)

    def last_rows(i, at):
        return ends[i, :, pl.ds(pl.multiple_of(at, LANES), LANES)].astype(jnp.float32)

    def pack_kv():
        half = kv_out.shape[1]

        @pl.loop(0, half // width)
        def _(c):
            for t in range(tiles):
                at = c * width + t * LANES
                packed = jnp.where(
                    row < 2, pltpu.roll(last_rows(0, at), 2, 0),
                    jnp.where(
                        row < 4, pltpu.roll(last_rows(1, at), 4, 0),
                        jnp.where(
                            row < 6, pltpu.roll(last_rows(0, at + half), 6, 0),
                            last_rows(1, at + half))))
                kv_out[:, pl.ds(pl.multiple_of(at, LANES), LANES)] = packed.astype(jnp.bfloat16)

    def pack_q():
        fourth = q_out.shape[1]

        @pl.loop(0, fourth // width)
        def _(c):
            for t in range(tiles):
                at = c * width + t * LANES
                packed = last_rows(2, at + 3 * fourth)
                for m in range(3):
                    packed = jnp.where(
                        row // 2 == m, pltpu.roll(last_rows(2, at + m * fourth), 2 + 2 * m, 0),
                        packed)
                q_out[:, pl.ds(pl.multiple_of(at, LANES), LANES)] = packed.astype(jnp.bfloat16)

    def taps_of(i, cols):
        return [feat[i, pl.ds(j, 1), cols] for j in range(FEAT)]

    def kv_rims(c, t):
        per_half = chunks // 2
        upper = c >= per_half
        at = lax.rem(c, per_half) * width + t * LANES
        x = kv_in[:, pl.ds(pl.multiple_of(at, LANES), LANES)].astype(jnp.float32)
        return (jnp.where(upper, pltpu.roll(x, 2, 0), pltpu.roll(x, 6, 0)),
                jnp.where(upper, x, pltpu.roll(x, 4, 0)))

    def q_rim(c, t):
        per_fourth = chunks // 4
        m = c // per_fourth
        at = lax.rem(c, per_fourth) * width + t * LANES
        x = q_in[:, pl.ds(pl.multiple_of(at, LANES), LANES)].astype(jnp.float32)
        rim = x
        for i in range(3):
            rim = jnp.where(m == i, pltpu.roll(x, 6 - 2 * i, 0), rim)
        return rim

    def columns(c, t):
        return pl.ds(pl.multiple_of(c * width + t * LANES, LANES), LANES)

    def gate(c, t, first, count, k_rim, v_rim):
        cols = columns(c, t)
        part, lanes = pl.ds(first, count), pl.ds(t * LANES, LANES)
        k_feat = featurize(kv[2 * c, part, lanes], k_rim, taps_of(1, cols))
        v_feat = featurize(kv[2 * c + 1, part, lanes], v_rim, taps_of(2, cols))
        return (k_feat * v_feat).astype(jnp.bfloat16)

    ends_wait(0, 2)
    pack_kv()

    if line:
        @pl.when(turns)
        def _():
            pl.semaphore_wait(barrier, 2)

        @pl.when(jnp.logical_and(has_right, jnp.logical_not(turns)))
        def _():
            pl.semaphore_wait(barrier, 1)
    else:
        @pl.when(has_right)
        def _():
            pl.semaphore_wait(barrier, 1)

    @pl.when(has_right)
    def _():
        kv_copy().start()

    ends_wait(2, 1)
    pack_q()

    @pl.when(has_right)
    def _():
        q_copy().start()

    zeros = jnp.zeros((8, LANES), jnp.float32)
    par_copy(0).wait()
    for c in range(EARLY):
        if c == 0:
            kv_wait(0, 1, 0)
        elif c == 1:
            kv_wait(1, EARLY - 1, 1)
        for t in range(tiles):
            lanes = pl.ds(t * LANES, LANES)
            gated[c, BODY, lanes] = gate(c, t, 0, rows, zeros, zeros)[16:]
            if c == 0 and t % 2 == 1:
                @pl.when(plain)
                def _():
                    piece(0, 0, BODY, pl.ds((t - 1) * LANES, 2 * LANES), 3).start()

        if hops:
            if c < hops:
                @pl.when(jnp.logical_and(turns, c < behind))
                def _():
                    hop_copy(c).start()

            if 0 < c <= hops:
                @pl.when(jnp.logical_and(turns, behind == c))
                def _():
                    for h in range(c - 1):
                        hop_copy(h).wait_send()

            if c == hops:
                @pl.when(jnp.logical_and(turns, behind > c))
                def _():
                    for h in range(c):
                        hop_copy(h).wait_send()

            if c > 0:
                @pl.when(jnp.logical_and(turns, c >= jnp.minimum(behind, hops)))
                def _():
                    piece(c, c // 2, BODY, send=3).start()

        if c > 0:
            @pl.when(plain)
            def _():
                piece(c, c // 2, BODY, send=3).start()

    @pl.loop(EARLY, chunks)
    def _(c):
        kv_load(0, c, 1).start()
        kv_load(1, c, 1).start()

    @pl.when(has_left)
    def _():
        kv_copy().wait_recv()

    @pl.when(jnp.logical_not(has_left))
    def _():
        kv_in[...] = jnp.zeros_like(kv_in)
        q_in[...] = jnp.zeros_like(q_in)

        @pl.loop(0, chunks)
        def _(c):
            prev[c] = jnp.zeros((rows, width), jnp.bfloat16)

    for c in range(EARLY):
        for t in range(tiles):
            gated[c, pl.ds(0, 16), pl.ds(t * LANES, LANES)] = gate(
                c, t, 0, 16, *kv_rims(c, t))

        @pl.when(has_right)
        def _():
            piece(c, c // 2, HEAD, send=4).start()

    par_copy(1).start()
    par_copy(2).start()

    @pl.loop(0, chunks)
    def _(c):
        q_load(c).start()

    kv_wait(EARLY, chunks - EARLY, 1)
    @pl.loop(EARLY, chunks)
    def _(c):
        for t in range(tiles):
            gated[c, :, pl.ds(t * LANES, LANES)] = gate(c, t, 0, rows, *kv_rims(c, t))

        @pl.when(has_right)
        def _():
            piece(c, jnp.where(c == last, pairs + 1, c // 2)).start()

    par_copy(1).wait()
    par_copy(2).wait()
    taps = lax.broadcasted_iota(jnp.int32, (FILT, 2 * LANES), 0)
    place = lax.broadcasted_iota(jnp.int32, (FILT, 2 * LANES), 1)
    total = taps + place
    for b in range(SUB):
        onehot = jnp.where(total == FILT + b, 1.0, 0.0).astype(jnp.bfloat16)
        moved = jnp.dot(filt[...], onehot, preferred_element_type=jnp.float32)
        for r in range(2):
            toep[r, pl.ds(b, groups, stride=SUB), :] = moved[:, r * LANES:(r + 1) * LANES]

    def operand(c, t):
        first = pl.multiple_of((c * tiles + t) * LANES, LANES)
        left_part = toep[0, pl.ds(first, LANES), :].astype(jnp.bfloat16)
        right_part = toep[1, pl.ds(first, LANES), :].astype(jnp.bfloat16)
        return left_part, right_part

    def factors(c, t):
        cols, lanes = columns(c, t), pl.ds(t * LANES, LANES)
        q_feat = featurize(q[c, :, lanes], q_rim(c, t), taps_of(0, cols))
        return q_feat, skip[:, cols] * gated[c, :, lanes].astype(jnp.float32)

    def mix(c):
        for t in range(tiles):
            lanes = pl.ds(t * LANES, LANES)
            window = jnp.concatenate([prev[c, :, lanes], gated[c, :, lanes]], axis=0)
            left_part, right_part = operand(c, t)
            lhs = jnp.concatenate([left_part, right_part[:, :SUB]], axis=1)
            conv = convolve(lhs, window)
            q_feat, direct = factors(c, t)
            mixed[c, :, lanes] = (q_feat * (conv + direct)).astype(jnp.bfloat16)

    @pl.when(has_left)
    def _():
        q_copy().wait_recv()

    pltpu.make_async_copy(q, q, in_sem.at[0]).wait()
    for h in range(hops):
        carry(h)

    @pl.loop(0, pairs)
    def _(i):
        @pl.when(has_left)
        def _():
            arrived(2 * i, 2, i)

        @pl.loop(2 * i, 2 * i + 2)
        def _(c):
            mix(c)

    for c in range(2 * pairs, last):
        @pl.when(has_left)
        def _():
            arrived(c, 1, pairs)

        mix(c)

    for t in range(tiles):
        lanes = pl.ds(t * LANES, LANES)
        left_part, right_part = operand(last, t)
        end_lhs[t, :, :LANES] = left_part
        end_lhs[t, :, LANES:] = right_part
        end_q[:, lanes], end_direct[:, lanes] = factors(last, t)
        end_window[pl.ds(rows, rows), lanes] = gated[last, :, lanes]

    @pl.when(has_left)
    def _():
        arrived(last, 1, pairs + 1)

    end_window[pl.ds(0, rows), :] = prev[last]

    @pl.when(has_right)
    def _():
        kv_copy().wait_send()
        q_copy().wait_send()
        sent(gated.at[pl.ds(EARLY, chunks - EARLY)], 0)
        sent(gated.at[pl.ds(0, EARLY), HEAD], 4)

    @pl.when(plain)
    def _():
        sent(gated.at[pl.ds(0, EARLY), BODY], 3)

    if hops:
        for b in range(1, hops + 1):
            held = behind == b if b < hops else behind >= b

            @pl.when(jnp.logical_and(turns, held))
            def _():
                sent(gated.at[pl.ds(0, EARLY - b), BODY], 3)

            @pl.when(jnp.logical_and(carries, held))
            def _():
                sent(hop.at[pl.ds(0, b), BODY], 5)

            @pl.when(jnp.logical_and(turns, behind == b))
            def _():
                hop_copy(b - 1).wait_send()


def drain(mixed, window, lhs, q_feat, direct, out_hbm, ending, sem):
    chunks, _, width = mixed.shape
    last = chunks - 1

    def lanes_of(t, base=0):
        return slice(base + t * LANES, base + (t + 1) * LANES)

    for c in range(last):
        pltpu.make_async_copy(
            mixed.at[c], out_hbm.at[:, c * width:(c + 1) * width], sem.at[0]).start()
    for t in range(width // LANES):
        lanes = lanes_of(t)
        conv = convolve(lhs[t, :, :FILT + SUB], window[:, lanes])
        ending[:, lanes] = (q_feat[:, lanes] * (conv + direct[:, lanes])).astype(jnp.bfloat16)
        pltpu.make_async_copy(
            ending.at[:, lanes], out_hbm.at[:, lanes_of(t, last * width)], sem.at[1]).start()
    done = mixed.at[pl.ds(0, last)]
    pltpu.make_async_copy(done, done, sem.at[0]).wait()
    pltpu.make_async_copy(ending, ending, sem.at[1]).wait()


def shards(n, line, q_stream, k_stream, v_stream, feat_filter, long_filter, skip_gain):
    rows, channels = q_stream.shape
    groups = long_filter.shape[0]
    chunks = channels // CHUNK
    cut = pltpu.VMEM((chunks, rows, CHUNK), jnp.bfloat16)
    dma = pltpu.SemaphoreType.DMA
    hops = HOPS if line else 0
    arrivals = 4 + (chunks - 1) // 2
    hops = max(hops, 1)
    tiles = CHUNK // LANES
    parts = pl.pallas_call(
        functools.partial(kernel, n, line),
        out_shape=(
            cut, pltpu.VMEM((2 * rows, CHUNK), jnp.bfloat16),
            pltpu.VMEM((tiles, LANES, 2 * LANES), jnp.bfloat16),
            pltpu.VMEM((rows, CHUNK), jnp.float32), pltpu.VMEM((rows, CHUNK), jnp.float32)),
        in_specs=[pl.BlockSpec(memory_space=pltpu.HBM)] * 6,
        out_specs=[pl.BlockSpec(memory_space=pltpu.VMEM)] * 5,
        scratch_shapes=[
            cut, pltpu.VMEM((2 * chunks, rows, CHUNK), jnp.bfloat16),
            pltpu.VMEM(feat_filter.shape, jnp.float32),
            pltpu.VMEM(long_filter.shape, jnp.bfloat16),
            pltpu.VMEM((1, channels), jnp.float32),
            pltpu.VMEM((3, 8, channels), jnp.bfloat16),
            pltpu.VMEM((8, channels // 2), jnp.bfloat16),
            pltpu.VMEM((8, channels // 2), jnp.bfloat16),
            pltpu.VMEM((8, channels // 4), jnp.bfloat16),
            pltpu.VMEM((8, channels // 4), jnp.bfloat16),
            cut, cut,
            pltpu.VMEM((2, groups * SUB, LANES), jnp.float32),
            pltpu.VMEM((hops, rows, CHUNK), jnp.bfloat16),
            dma((2,)), dma((2,)), dma((1,)), dma((5 + (hops if line else 0),)), dma((arrivals,)), dma((hops,)),
        ],
        compiler_params=pltpu.CompilerParams(
            collective_id=0, has_side_effects=True, vmem_limit_bytes=GRANT),
    )(q_stream, k_stream, v_stream, feat_filter, long_filter, skip_gain.reshape(1, channels))
    return pl.pallas_call(
        drain,
        out_shape=jax.ShapeDtypeStruct((rows, channels), jnp.bfloat16),
        in_specs=[pl.BlockSpec(memory_space=pltpu.VMEM)] * 5,
        out_specs=pl.BlockSpec(memory_space=pl.ANY),
        scratch_shapes=[pltpu.VMEM((rows, CHUNK), jnp.bfloat16), dma((2,))],
        compiler_params=pltpu.CompilerParams(vmem_limit_bytes=8 << 20),
    )(*parts)


def solution(mesh):
    n = mesh.shape["seq"]
    rows = P(("rep", "seq"), None)
    return jax.shard_map(
        functools.partial(shards, n, row_of(mesh)), mesh=mesh,
        in_specs=(rows, rows, rows, P(), P(), P()), out_specs=rows, check_vma=False)
```

```python
import functools

import jax
import jax.numpy as jnp
from jax import lax
from jax.experimental import pallas as pl
from jax.experimental.pallas import tpu as pltpu
from jax.sharding import PartitionSpec as P

GROUP_CH = 16
FILT = 128
FEAT = 3
LANES = 128
SUB = 16
CHUNK = 512
EARLY = 4
HOPS = 3
AIDE = 0
GRANT = 59 << 20
MESH = pl.DeviceIdType.MESH


def shifted(rim, x):
    ext = jnp.concatenate([rim, x], axis=0)
    return pltpu.roll(ext, 1, 0)[8:], pltpu.roll(ext, 2, 0)[8:]


def featurize(x, rim, taps):
    x = x.astype(jnp.float32)
    one, two = shifted(rim, x)
    return taps[0] * x + taps[1] * one + taps[2] * two


def row_of(mesh):
    ring = mesh.devices.reshape(-1, mesh.shape["seq"])[0]
    at = [getattr(d, "coords", None) for d in ring]
    if None in at:
        return 0
    apart = [sum(p != q for p, q in zip(a, b)) for a, b in zip(at, at[1:])]
    turns = [i + 1 for i, axes in enumerate(apart) if axes > 1]
    row = turns[0] if turns else 0
    return row if row > 2 and len(ring) % row == 0 else 0


def convolve(lhs, window):
    rows = window.shape[0] - FILT
    blocks = rows // SUB
    depth = FILT + SUB
    lane_group = lax.broadcasted_iota(jnp.int32, (SUB, LANES), 1) // GROUP_CH
    rhs = jnp.concatenate([window[a * SUB:a * SUB + depth] for a in range(blocks)], axis=1)
    every = jnp.dot(lhs, rhs, preferred_element_type=jnp.float32)
    conv = []
    for a in range(blocks):
        mine = every[:SUB, a * LANES:(a + 1) * LANES]
        for g in range(1, LANES // GROUP_CH):
            mine = jnp.where(
                lane_group == g,
                every[g * SUB:(g + 1) * SUB, a * LANES:(a + 1) * LANES], mine)
        conv.append(mine)
    return jnp.concatenate(conv, axis=0)


def kernel(
    n, line, q_hbm, k_hbm, v_hbm, feat_hbm, long_hbm, skip_hbm,
    mixed, end_window, end_lhs, end_q, end_direct, end_taps,
    q, kv, feat, filt, skip, ends, rim_out, rim_in, tops, gated, prev, toep,
    hop, in_sem, send_sem, recv_sem,
):
    chunks, rows, width = gated.shape
    tiles = width // LANES
    groups = filt.shape[0]
    channels = chunks * width
    me = lax.axis_index("seq")
    right, left = lax.rem(me + 1, n), lax.rem(me + n - 1, n)
    has_left, has_right = me > 0, me < n - 1

    barrier = pltpu.get_barrier_semaphore()

    @pl.when(has_left)
    def _():
        pl.semaphore_signal(barrier, inc=1, device_id={"seq": left}, device_id_type=MESH)

    hops = hop.shape[0] if line else 0
    half = channels // 2
    if line:
        spot, level = lax.rem(me, line), me // line
        behind = n // line - 1 - level
        turns = jnp.logical_and(spot == line - 1, has_right)
        carries = jnp.logical_and(spot == AIDE, behind > 0)
        plain = jnp.logical_and(has_right, jnp.logical_not(turns))

        @pl.when(carries)
        def _():
            pl.semaphore_signal(
                barrier, inc=1, device_id={"seq": me + line - 1 - AIDE}, device_id_type=MESH)

    else:
        plain = has_right

    streams = (k_hbm, v_hbm, q_hbm)

    def end_copy(i):
        return pltpu.make_async_copy(
            streams[i].at[pl.ds(rows - 8, 8)], ends.at[i], in_sem.at[0])

    def cols_of(c):
        return pl.ds(pl.multiple_of(c * width, width), width)

    def kv_load(i, c):
        return pltpu.make_async_copy(
            streams[i].at[:, cols_of(c)], kv.at[2 * c + i], in_sem.at[2])

    def loaded(part, slot):
        pltpu.make_async_copy(part, part, in_sem.at[slot]).wait()

    def q_load(c):
        return pltpu.make_async_copy(q_hbm.at[:, cols_of(c)], q.at[c], in_sem.at[0])

    params = ((feat_hbm, feat, 1), (long_hbm, filt, 1), (skip_hbm, skip, 2))

    def par_copy(i):
        src, dst, slot = params[i]
        return pltpu.make_async_copy(src, dst, in_sem.at[slot])

    for i in range(3):
        end_copy(i).start()
    par_copy(0).start()
    for c in range(EARLY):
        kv_load(0, c).start()
        kv_load(1, c).start()

    def remote(src, dst, send, recv, to=right):
        return pltpu.make_async_remote_copy(
            src_ref=src, dst_ref=dst, send_sem=send_sem.at[send], recv_sem=recv,
            device_id={"seq": to}, device_id_type=MESH)

    def rim_copy():
        return remote(rim_out, rim_in, 1, recv_sem.at[0])

    last = chunks - 1
    quads, spare = (last - 1) // 4, (last - 1) % 4
    near = 1 + quads + (1 if spare else 0)
    hop_slot = near + 2

    def slot(c):
        return jnp.where(c == last, near + 1, jnp.where(c == last - 1, near, 1 + c // 4))

    def piece(c, part=slice(None), lanes=slice(None)):
        return remote(
            gated.at[c, part, lanes], prev.at[c, part, lanes], 0, recv_sem.at[slot(c)])

    def sent(part, slot):
        pltpu.make_async_copy(part, part, send_sem.at[slot]).wait()

    def arrived(first, count, group):
        part = prev.at[pl.ds(first, count)]
        pltpu.make_async_copy(part, part, recv_sem.at[group]).wait()

    HEAD, BODY = pl.ds(0, 16), pl.ds(16, rows - 16)

    def hop_copy(h):
        return remote(
            gated.at[h, BODY], hop.at[h, BODY], jnp.where(h == behind - 1, 0, 2),
            recv_sem.at[hop_slot],
            jnp.maximum(me - line + 1 + AIDE, 0))

    def forward_copy(h):
        return remote(
            hop.at[h, BODY], prev.at[h, BODY], 2, recv_sem.at[slot(h)],
            jnp.minimum(me + line - AIDE, n - 1))

    def held(b):
        return behind == b if b < hops else behind >= b

    def carry(b):
        @pl.when(jnp.logical_and(carries, held(b)))
        def _():
            part = hop.at[pl.ds(0, b), BODY]
            pltpu.make_async_copy(part, part, recv_sem.at[hop_slot]).wait()
            for h in range(b):
                forward_copy(h).start()

    row = lax.broadcasted_iota(jnp.int32, (8, LANES), 0)

    def last_rows(i, at):
        return ends[i, :, pl.ds(pl.multiple_of(at, LANES), LANES)].astype(jnp.float32)

    def pack_kv():
        @pl.loop(0, half // width)
        def _(c):
            for t in range(tiles):
                at = c * width + t * LANES
                packed = jnp.where(
                    row < 2, pltpu.roll(last_rows(0, at), 2, 0),
                    jnp.where(
                        row < 4, pltpu.roll(last_rows(1, at), 4, 0),
                        jnp.where(
                            row < 6, pltpu.roll(last_rows(0, at + half), 6, 0),
                            last_rows(1, at + half))))
                rim_out[:, pl.ds(pl.multiple_of(at, LANES), LANES)] = packed.astype(jnp.bfloat16)

    def pack_q():
        eighth = channels // 8

        @pl.loop(0, eighth // width)
        def _(c):
            for t in range(tiles):
                at = c * width + t * LANES
                packed = last_rows(2, at + 6 * eighth)
                for m in range(8):
                    if m != 6:
                        moved = pltpu.roll(last_rows(2, at + m * eighth), (m + 2) % 8, 0)
                        packed = jnp.where(row == m, moved, packed)
                rim_out[:, pl.ds(pl.multiple_of(half + at, LANES), LANES)] = packed.astype(
                    jnp.bfloat16)

    def taps_of(i, cols):
        return [feat[i, pl.ds(j, 1), cols] for j in range(FEAT)]

    def kv_rims(c, t):
        per_half = chunks // 2
        upper = c >= per_half
        at = lax.rem(c, per_half) * width + t * LANES
        x = rim_in[:, pl.ds(pl.multiple_of(at, LANES), LANES)].astype(jnp.float32)
        return (jnp.where(upper, pltpu.roll(x, 2, 0), pltpu.roll(x, 6, 0)),
                jnp.where(upper, x, pltpu.roll(x, 4, 0)))

    def q_rim(c, t, final=False):
        per_eighth = chunks // 8
        at = half + lax.rem(c, per_eighth) * width + t * LANES
        x = rim_in[:, pl.ds(pl.multiple_of(at, LANES), LANES)].astype(jnp.float32)
        two = jnp.sum(jnp.where(row == c // per_eighth, x, 0.0), axis=0, keepdims=True)
        rim = jnp.where(row == 6, two, 0.0)
        if final:
            return rim
        one = prev[c, HEAD, pl.ds(t * LANES, LANES)].astype(jnp.float32)[:1]
        return jnp.where(row == 7, one, rim)

    def columns(c, t):
        return pl.ds(pl.multiple_of(c * width + t * LANES, LANES), LANES)

    def gate(c, t, first, count, k_rim, v_rim):
        cols = columns(c, t)
        part, lanes = pl.ds(first, count), pl.ds(t * LANES, LANES)
        k_feat = featurize(kv[2 * c, part, lanes], k_rim, taps_of(1, cols))
        v_feat = featurize(kv[2 * c + 1, part, lanes], v_rim, taps_of(2, cols))
        return (k_feat * v_feat).astype(jnp.bfloat16)

    row16 = lax.broadcasted_iota(jnp.int32, (16, LANES), 0)

    def put_head(c, t, block):
        at = c * width + t * LANES
        tops[:, columns(c, t)] = block[:1].astype(jnp.float32)
        gated[c, HEAD, pl.ds(t * LANES, LANES)] = jnp.where(
            row16 == 0, last_rows(2, at)[7:], block.astype(jnp.float32)).astype(jnp.bfloat16)

    def own(c, t):
        lanes = pl.ds(t * LANES, LANES)
        head = jnp.where(
            row16 == 0, tops[:, columns(c, t)], gated[c, HEAD, lanes].astype(jnp.float32))
        return jnp.concatenate([head.astype(jnp.bfloat16), gated[c, BODY, lanes]], axis=0)

    loaded(ends, 0)
    pack_kv()
    pack_q()

    if line:
        @pl.when(turns)
        def _():
            pl.semaphore_wait(barrier, 2)

        @pl.when(jnp.logical_and(has_right, jnp.logical_not(turns)))
        def _():
            pl.semaphore_wait(barrier, 1)
    else:
        @pl.when(has_right)
        def _():
            pl.semaphore_wait(barrier, 1)

    @pl.when(has_right)
    def _():
        rim_copy().start()

    zeros = jnp.zeros((8, LANES), jnp.float32)
    par_copy(0).wait()
    loaded(kv.at[pl.ds(0, 2 * EARLY)], 2)
    for c in range(EARLY):
        for t in range(tiles):
            lanes = pl.ds(t * LANES, LANES)
            gated[c, BODY, lanes] = gate(c, t, 0, rows, zeros, zeros)[16:]
            if c == 0 and t % 2 == 1:
                @pl.when(plain)
                def _():
                    piece(0, BODY, pl.ds((t - 1) * LANES, 2 * LANES)).start()

        if hops:
            if c < hops:
                @pl.when(jnp.logical_and(turns, c < behind))
                def _():
                    hop_copy(c).start()

            if 1 < c <= hops:
                @pl.when(jnp.logical_and(turns, behind == c))
                def _():
                    sent(gated.at[pl.ds(0, c - 1), BODY], 2)

            if c == hops:
                @pl.when(jnp.logical_and(turns, behind > c))
                def _():
                    sent(gated.at[pl.ds(0, c), BODY], 2)

            if c > 0:
                @pl.when(jnp.logical_and(turns, c >= jnp.minimum(behind, hops)))
                def _():
                    piece(c, BODY).start()

        if c > 0:
            @pl.when(plain)
            def _():
                piece(c, BODY).start()

    @pl.loop(EARLY, chunks)
    def _(c):
        kv_load(0, c).start()
        kv_load(1, c).start()

    @pl.when(has_left)
    def _():
        rim_copy().wait_recv()

    @pl.when(jnp.logical_not(has_left))
    def _():
        rim_in[...] = jnp.zeros_like(rim_in)

        @pl.loop(0, chunks)
        def _(c):
            prev[c] = jnp.zeros((rows, width), jnp.bfloat16)

    for c in range(EARLY):
        for t in range(tiles):
            put_head(c, t, gate(c, t, 0, 16, *kv_rims(c, t)))

        @pl.when(has_right)
        def _():
            piece(c, HEAD).start()

    par_copy(1).start()

    @pl.loop(0, chunks)
    def _(c):
        q_load(c).start()

    loaded(kv.at[pl.ds(2 * EARLY, 2 * (chunks - EARLY))], 2)
    par_copy(2).start()

    @pl.loop(EARLY, chunks)
    def _(c):
        for t in range(tiles):
            block = gate(c, t, 0, rows, *kv_rims(c, t))
            put_head(c, t, block[:16])
            gated[c, BODY, pl.ds(t * LANES, LANES)] = block[16:]

        @pl.when(has_right)
        def _():
            piece(c).start()

    par_copy(1).wait()
    par_copy(2).wait()
    taps = lax.broadcasted_iota(jnp.int32, (FILT, 2 * LANES), 0)
    place = lax.broadcasted_iota(jnp.int32, (FILT, 2 * LANES), 1)
    total = taps + place
    for b in range(SUB):
        onehot = jnp.where(total == FILT + b, 1.0, 0.0).astype(jnp.bfloat16)
        moved = jnp.dot(filt[...], onehot, preferred_element_type=jnp.float32)
        for r in range(2):
            toep[r, pl.ds(b, groups, stride=SUB), :] = moved[:, r * LANES:(r + 1) * LANES]

    def operand(c, t):
        first = pl.multiple_of((c * tiles + t) * LANES, LANES)
        left_part = toep[0, pl.ds(first, LANES), :].astype(jnp.bfloat16)
        right_part = toep[1, pl.ds(first, LANES), :].astype(jnp.bfloat16)
        return left_part, right_part

    def factors(c, t, mine, rim):
        cols, lanes = columns(c, t), pl.ds(t * LANES, LANES)
        q_feat = featurize(q[c, :, lanes], rim, taps_of(0, cols))
        return q_feat, skip[:, cols] * mine.astype(jnp.float32)

    def mix(c):
        for t in range(tiles):
            lanes = pl.ds(t * LANES, LANES)
            mine = own(c, t)
            window = jnp.concatenate([prev[c, :, lanes], mine], axis=0)
            left_part, right_part = operand(c, t)
            lhs = jnp.concatenate([left_part, right_part[:, :SUB]], axis=1)
            conv = convolve(lhs, window)
            q_feat, direct = factors(c, t, mine, q_rim(c, t))
            mixed[c, :, lanes] = (q_feat * (conv + direct)).astype(jnp.bfloat16)

    loaded(q, 0)
    for b in range(1, hops + 1):
        carry(b)

    def stage(first, count, group):
        @pl.when(has_left)
        def _():
            arrived(first, count, group)

        @pl.loop(first, first + count)
        def _(c):
            mix(c)

    @pl.loop(0, quads)
    def _(i):
        stage(4 * i, 4, 1 + i)

    if spare:
        stage(4 * quads, spare, 1 + quads)
    stage(last - 1, 1, near)

    first = columns(last, 0).start
    end_taps[pl.ds(0, 2), :] = feat[0, pl.ds(1, 2), pl.ds(first, width)]
    for t in range(tiles):
        lanes = pl.ds(t * LANES, LANES)
        left_part, right_part = operand(last, t)
        end_lhs[t, :, :LANES] = left_part
        end_lhs[t, :, LANES:] = right_part
        mine = own(last, t)
        end_q[:, lanes], end_direct[:, lanes] = factors(last, t, mine, q_rim(last, t, True))
        end_window[pl.ds(rows, rows), lanes] = mine

    @pl.when(has_left)
    def _():
        arrived(last, 1, near + 1)

    end_window[pl.ds(0, rows), :] = prev[last]

    @pl.when(has_right)
    def _():
        rim_copy().wait_send()

    @pl.when(plain)
    def _():
        sent(gated, 0)

    def mostly(b):
        count = (chunks * rows - b * (rows - 16)) * width // (2 * LANES)
        sent(toep.at[0, pl.ds(0, count)], 0)

    for b in range(1, hops + 1):
        @pl.when(jnp.logical_and(turns, behind == b))
        def _():
            mostly(b - 1)

        @pl.when(jnp.logical_and(carries, held(b)))
        def _():
            sent(hop.at[pl.ds(0, b), BODY], 2)

    if hops:
        @pl.when(jnp.logical_and(turns, behind > hops))
        def _():
            mostly(hops)


def drain(mixed, window, lhs, q_feat, direct, taps, out_hbm, ending, sem):
    chunks, _, width = mixed.shape
    last = chunks - 1
    row = lax.broadcasted_iota(jnp.int32, (16, LANES), 0)

    def lanes_of(t, base=0):
        return slice(base + t * LANES, base + (t + 1) * LANES)

    for c in range(last):
        pltpu.make_async_copy(
            mixed.at[c], out_hbm.at[:, c * width:(c + 1) * width], sem.at[0]).start()
    for t in range(width // LANES):
        lanes = lanes_of(t)
        conv = convolve(lhs[t, :, :FILT + SUB], window[:, lanes])
        more = jnp.where(
            row == 0, taps[:1, lanes], jnp.where(row == 1, taps[1:2, lanes], 0.0))
        more = more * window[:16, lanes].astype(jnp.float32)[:1]
        scale = jnp.concatenate([q_feat[:16, lanes] + more, q_feat[16:, lanes]], axis=0)
        ending[:, lanes] = (scale * (conv + direct[:, lanes])).astype(jnp.bfloat16)
        pltpu.make_async_copy(
            ending.at[:, lanes], out_hbm.at[:, lanes_of(t, last * width)], sem.at[0]).start()
    pltpu.make_async_copy(mixed, mixed, sem.at[0]).wait()


def shards(n, line, q_stream, k_stream, v_stream, feat_filter, long_filter, skip_gain):
    rows, channels = q_stream.shape
    groups = long_filter.shape[0]
    chunks = channels // CHUNK
    cut = pltpu.VMEM((chunks, rows, CHUNK), jnp.bfloat16)
    rim = pltpu.VMEM((8, channels // 2 + channels // 8), jnp.bfloat16)
    dma = pltpu.SemaphoreType.DMA
    hops = HOPS if line else 0
    arrivals = 4 + (chunks + 1) // 4
    hops = max(hops, 1)
    tiles = CHUNK // LANES
    parts = pl.pallas_call(
        functools.partial(kernel, n, line),
        out_shape=(
            cut, pltpu.VMEM((2 * rows, CHUNK), jnp.bfloat16),
            pltpu.VMEM((tiles, LANES, 2 * LANES), jnp.bfloat16),
            pltpu.VMEM((rows, CHUNK), jnp.float32), pltpu.VMEM((rows, CHUNK), jnp.float32),
            pltpu.VMEM((8, CHUNK), jnp.float32)),
        in_specs=[pl.BlockSpec(memory_space=pltpu.HBM)] * 6,
        out_specs=[pl.BlockSpec(memory_space=pltpu.VMEM)] * 6,
        scratch_shapes=[
            cut, pltpu.VMEM((2 * chunks, rows, CHUNK), jnp.bfloat16),
            pltpu.VMEM(feat_filter.shape, jnp.float32),
            pltpu.VMEM(long_filter.shape, jnp.bfloat16),
            pltpu.VMEM((1, channels), jnp.float32),
            pltpu.VMEM((3, 8, channels), jnp.bfloat16),
            rim, rim,
            pltpu.VMEM((1, channels), jnp.float32),
            cut, cut,
            pltpu.VMEM((2, groups * SUB, LANES), jnp.float32),
            pltpu.VMEM((hops, rows, CHUNK), jnp.bfloat16),
            dma((3,)), dma((3,)), dma((arrivals,)),
        ],
        compiler_params=pltpu.CompilerParams(
            collective_id=0, has_side_effects=True, vmem_limit_bytes=GRANT),
    )(q_stream, k_stream, v_stream, feat_filter, long_filter, skip_gain.reshape(1, channels))
    return pl.pallas_call(
        drain,
        out_shape=jax.ShapeDtypeStruct((rows, channels), jnp.bfloat16),
        in_specs=[pl.BlockSpec(memory_space=pltpu.VMEM)] * 6,
        out_specs=pl.BlockSpec(memory_space=pl.ANY),
        scratch_shapes=[pltpu.VMEM((rows, CHUNK), jnp.bfloat16), dma((1,))],
        compiler_params=pltpu.CompilerParams(vmem_limit_bytes=8 << 20),
    )(*parts)


def solution(mesh):
    n = mesh.shape["seq"]
    rows = P(("rep", "seq"), None)
    return jax.shard_map(
        functools.partial(shards, n, row_of(mesh)), mesh=mesh,
        in_specs=(rows, rows, rows, P(), P(), P()), out_specs=rows, check_vma=False)
```

```python
import functools

import jax
import jax.numpy as jnp
from jax import lax
from jax.experimental import pallas as pl
from jax.experimental.pallas import tpu as pltpu
from jax.sharding import PartitionSpec as P

GROUP_CH = 16
FILT = 128
FEAT = 3
LANES = 128
SUB = 16
CHUNK = 512
EARLY = 4
HOPS = 3
AIDE = 0
GRANT = 59 << 20
MESH = pl.DeviceIdType.MESH


def shifted(rim, x):
    ext = jnp.concatenate([rim, x], axis=0)
    return pltpu.roll(ext, 1, 0)[8:], pltpu.roll(ext, 2, 0)[8:]


def featurize(x, rim, taps):
    x = x.astype(jnp.float32)
    one, two = shifted(rim, x)
    return taps[0] * x + taps[1] * one + taps[2] * two


def row_of(mesh):
    ring = mesh.devices.reshape(-1, mesh.shape["seq"])[0]
    at = [getattr(d, "coords", None) for d in ring]
    if None in at:
        return 0
    apart = [sum(p != q for p, q in zip(a, b)) for a, b in zip(at, at[1:])]
    turns = [i + 1 for i, axes in enumerate(apart) if axes > 1]
    row = turns[0] if turns else 0
    return row if row > 2 and len(ring) % row == 0 else 0


def convolve(lhs, window):
    rows = window.shape[0] - FILT
    blocks = rows // SUB
    depth = FILT + SUB
    lane_group = lax.broadcasted_iota(jnp.int32, (SUB, LANES), 1) // GROUP_CH
    rhs = jnp.concatenate([window[a * SUB:a * SUB + depth] for a in range(blocks)], axis=1)
    every = jnp.dot(lhs, rhs, preferred_element_type=jnp.float32)
    conv = []
    for a in range(blocks):
        mine = every[:SUB, a * LANES:(a + 1) * LANES]
        for g in range(1, LANES // GROUP_CH):
            mine = jnp.where(
                lane_group == g,
                every[g * SUB:(g + 1) * SUB, a * LANES:(a + 1) * LANES], mine)
        conv.append(mine)
    return jnp.concatenate(conv, axis=0)


def kernel(
    n, line, q_hbm, k_hbm, v_hbm, feat_hbm, long_hbm, skip_hbm,
    mixed, end_window, end_lhs, end_q, end_direct, end_taps,
    q, kv, feat, filt, skip, ends, rim_out, rim_in, guest_in, tops, gated, prev, toep,
    hop, in_sem, send_sem, recv_sem, go,
):
    chunks, rows, width = gated.shape
    tiles = width // LANES
    groups = filt.shape[0]
    channels = chunks * width
    me = lax.axis_index("seq")
    right, left = lax.rem(me + 1, n), lax.rem(me + n - 1, n)
    has_left, has_right = me > 0, me < n - 1

    barrier = pltpu.get_barrier_semaphore()

    def greet(device):
        pl.semaphore_signal(barrier, inc=1, device_id={"seq": device}, device_id_type=MESH)

    if line:
        spot = lax.rem(me, line)
        host = jnp.logical_and(lax.rem(spot, 2) == 0, spot > 1)
        guest = jnp.logical_and(lax.rem(spot, 2) == 1, spot > 1)
        caller = jnp.logical_and(lax.rem(spot, 2) == 1, spot < line - 1)

        @pl.when(jnp.logical_and(has_left, jnp.logical_not(host)))
        def _():
            greet(left)

        @pl.when(caller)
        def _():
            greet(right)

        @pl.when(guest)
        def _():
            greet(jnp.maximum(me - 2, 0))

        @pl.when(host)
        def _():
            pl.semaphore_wait(barrier, 2)
            pl.semaphore_signal(go, inc=1, device_id={"seq": left}, device_id_type=MESH)
    else:
        @pl.when(has_left)
        def _():
            greet(left)

    hops = hop.shape[0] if line else 0
    half = channels // 2
    if line:
        level = me // line
        behind = n // line - 1 - level
        turns = jnp.logical_and(spot == line - 1, has_right)
        carries = jnp.logical_and(spot == AIDE, behind > 0)
        plain = jnp.logical_and(has_right, jnp.logical_not(turns))

        @pl.when(carries)
        def _():
            greet(jnp.minimum(me + line - 1 - AIDE, n - 1))
    else:
        plain = has_right

    streams = (k_hbm, v_hbm, q_hbm)

    def end_copy(i):
        return pltpu.make_async_copy(
            streams[i].at[pl.ds(rows - 8, 8)], ends.at[i], in_sem.at[0])

    def cols_of(c):
        return pl.ds(pl.multiple_of(c * width, width), width)

    def kv_load(i, c):
        return pltpu.make_async_copy(
            streams[i].at[:, cols_of(c)], kv.at[2 * c + i], in_sem.at[2])

    def loaded(part, slot):
        pltpu.make_async_copy(part, part, in_sem.at[slot]).wait()

    def q_load(c):
        return pltpu.make_async_copy(q_hbm.at[:, cols_of(c)], q.at[c], in_sem.at[0])

    params = ((feat_hbm, feat, 1), (long_hbm, filt, 1), (skip_hbm, skip, 2))

    def par_copy(i):
        src, dst, slot = params[i]
        return pltpu.make_async_copy(src, dst, in_sem.at[slot])

    for i in range(3):
        end_copy(i).start()
    par_copy(0).start()
    for c in range(EARLY):
        kv_load(0, c).start()
        kv_load(1, c).start()

    def remote(src, dst, send, recv, to=right):
        return pltpu.make_async_remote_copy(
            src_ref=src, dst_ref=dst, send_sem=send_sem.at[send], recv_sem=recv,
            device_id={"seq": to}, device_id_type=MESH)

    def rim_copy():
        return remote(rim_out, rim_in, 1, recv_sem.at[0])

    last = chunks - 1
    quads, spare = (last - 1) // 4, (last - 1) % 4
    near = 1 + quads + (1 if spare else 0)
    hop_slot = near + 2
    guest_slot = near + 3

    def slot(c):
        return jnp.where(c == last, near + 1, jnp.where(c == last - 1, near, 1 + c // 4))

    def guest_copy():
        return remote(
            rim_out, guest_in, 1, recv_sem.at[guest_slot], jnp.minimum(me + 2, n - 1))

    def pass_copy():
        return remote(guest_in, rim_in, 3, recv_sem.at[0], left)

    def piece(c, part=slice(None), lanes=slice(None)):
        return remote(
            gated.at[c, part, lanes], prev.at[c, part, lanes], 0, recv_sem.at[slot(c)])

    def sent(part, slot):
        pltpu.make_async_copy(part, part, send_sem.at[slot]).wait()

    def arrived(first, count, group):
        part = prev.at[pl.ds(first, count)]
        pltpu.make_async_copy(part, part, recv_sem.at[group]).wait()

    HEAD, BODY = pl.ds(0, 16), pl.ds(16, rows - 16)

    def hop_copy(h, lanes=slice(None), send=None):
        if send is None:
            send = jnp.where(h == behind - 1, 0, 2)
        return remote(
            gated.at[h, BODY, lanes], hop.at[h, BODY, lanes], send, recv_sem.at[hop_slot],
            jnp.maximum(me - line + 1 + AIDE, 0))

    SOON, LATE = pl.ds(0, 3 * width // 4), pl.ds(3 * width // 4, width // 4)

    def forward_copy(h):
        return remote(
            hop.at[h, BODY], prev.at[h, BODY], 2, recv_sem.at[slot(h)],
            jnp.minimum(me + line - AIDE, n - 1))

    def held(b):
        return behind == b if b < hops else behind >= b

    def carry(b):
        @pl.when(jnp.logical_and(carries, held(b)))
        def _():
            part = hop.at[pl.ds(0, b), BODY]
            pltpu.make_async_copy(part, part, recv_sem.at[hop_slot]).wait()
            for h in range(b):
                forward_copy(h).start()

    row = lax.broadcasted_iota(jnp.int32, (8, LANES), 0)

    def last_rows(i, at):
        return ends[i, :, pl.ds(pl.multiple_of(at, LANES), LANES)].astype(jnp.float32)

    def pack_kv():
        @pl.loop(0, half // width)
        def _(c):
            for t in range(tiles):
                at = c * width + t * LANES
                packed = jnp.where(
                    row < 2, pltpu.roll(last_rows(0, at), 2, 0),
                    jnp.where(
                        row < 4, pltpu.roll(last_rows(1, at), 4, 0),
                        jnp.where(
                            row < 6, pltpu.roll(last_rows(0, at + half), 6, 0),
                            last_rows(1, at + half))))
                rim_out[:, pl.ds(pl.multiple_of(at, LANES), LANES)] = packed.astype(jnp.bfloat16)

    def pack_q():
        eighth = channels // 8

        @pl.loop(0, eighth // width)
        def _(c):
            for t in range(tiles):
                at = c * width + t * LANES
                packed = last_rows(2, at + 6 * eighth)
                for m in range(8):
                    if m != 6:
                        moved = pltpu.roll(last_rows(2, at + m * eighth), (m + 2) % 8, 0)
                        packed = jnp.where(row == m, moved, packed)
                rim_out[:, pl.ds(pl.multiple_of(half + at, LANES), LANES)] = packed.astype(
                    jnp.bfloat16)

    def taps_of(i, cols):
        return [feat[i, pl.ds(j, 1), cols] for j in range(FEAT)]

    def kv_rims(c, t):
        per_half = chunks // 2
        upper = c >= per_half
        at = lax.rem(c, per_half) * width + t * LANES
        x = rim_in[:, pl.ds(pl.multiple_of(at, LANES), LANES)].astype(jnp.float32)
        return (jnp.where(upper, pltpu.roll(x, 2, 0), pltpu.roll(x, 6, 0)),
                jnp.where(upper, x, pltpu.roll(x, 4, 0)))

    def q_rim(c, t, final=False):
        per_eighth = chunks // 8
        at = half + lax.rem(c, per_eighth) * width + t * LANES
        x = rim_in[:, pl.ds(pl.multiple_of(at, LANES), LANES)].astype(jnp.float32)
        two = jnp.sum(jnp.where(row == c // per_eighth, x, 0.0), axis=0, keepdims=True)
        rim = jnp.where(row == 6, two, 0.0)
        if final:
            return rim
        one = prev[c, HEAD, pl.ds(t * LANES, LANES)].astype(jnp.float32)[:1]
        return jnp.where(row == 7, one, rim)

    def columns(c, t):
        return pl.ds(pl.multiple_of(c * width + t * LANES, LANES), LANES)

    def gate(c, t, first, count, k_rim, v_rim):
        cols = columns(c, t)
        part, lanes = pl.ds(first, count), pl.ds(t * LANES, LANES)
        k_feat = featurize(kv[2 * c, part, lanes], k_rim, taps_of(1, cols))
        v_feat = featurize(kv[2 * c + 1, part, lanes], v_rim, taps_of(2, cols))
        return (k_feat * v_feat).astype(jnp.bfloat16)

    row16 = lax.broadcasted_iota(jnp.int32, (16, LANES), 0)

    def put_head(c, t, block):
        at = c * width + t * LANES
        tops[:, columns(c, t)] = block[:1].astype(jnp.float32)
        gated[c, HEAD, pl.ds(t * LANES, LANES)] = jnp.where(
            row16 == 0, last_rows(2, at)[7:], block.astype(jnp.float32)).astype(jnp.bfloat16)

    def own(c, t):
        lanes = pl.ds(t * LANES, LANES)
        head = jnp.where(
            row16 == 0, tops[:, columns(c, t)], gated[c, HEAD, lanes].astype(jnp.float32))
        return jnp.concatenate([head.astype(jnp.bfloat16), gated[c, BODY, lanes]], axis=0)

    loaded(ends, 0)
    pack_kv()
    pack_q()

    if line:
        @pl.when(turns)
        def _():
            pl.semaphore_wait(barrier, 2)

        @pl.when(caller)
        def _():
            pl.semaphore_wait(barrier, 1)
            guest_copy().start()

        alone = jnp.logical_or(jnp.logical_or(turns, host), caller)

        @pl.when(jnp.logical_and(has_right, jnp.logical_not(alone)))
        def _():
            pl.semaphore_wait(barrier, 1)

        near_by = jnp.logical_and(has_right, jnp.logical_not(caller))
    else:
        near_by = has_right

        @pl.when(has_right)
        def _():
            pl.semaphore_wait(barrier, 1)

    @pl.when(near_by)
    def _():
        rim_copy().start()

    zeros = jnp.zeros((8, LANES), jnp.float32)
    par_copy(0).wait()
    loaded(kv.at[pl.ds(0, 2 * EARLY)], 2)
    for c in range(EARLY):
        for t in range(tiles):
            lanes = pl.ds(t * LANES, LANES)
            gated[c, BODY, lanes] = gate(c, t, 0, rows, zeros, zeros)[16:]
            if line and c == 0 and t == 1:
                @pl.when(caller)
                def _():
                    pl.semaphore_wait(go, 1)

            if c == 0 and t % 2 == 1:
                @pl.when(plain)
                def _():
                    piece(0, BODY, pl.ds((t - 1) * LANES, 2 * LANES)).start()

        if hops:
            if c < hops:
                halved = behind == 2 if c == 0 else False

                @pl.when(jnp.logical_and(
                    turns, jnp.logical_and(c < behind, jnp.logical_not(halved))))
                def _():
                    hop_copy(c).start()

                @pl.when(jnp.logical_and(turns, halved))
                def _():
                    hop_copy(c, SOON, 2).start()
                    hop_copy(c, LATE, 0).start()

            if 1 < c <= hops:
                @pl.when(jnp.logical_and(turns, behind == c))
                def _():
                    if c == 2:
                        sent(gated.at[0, BODY, SOON], 2)
                    else:
                        sent(gated.at[pl.ds(0, c - 1), BODY], 2)

            if c == hops:
                @pl.when(jnp.logical_and(turns, behind > c))
                def _():
                    sent(gated.at[pl.ds(0, c), BODY], 2)

            if c > 0:
                @pl.when(jnp.logical_and(turns, c >= jnp.minimum(behind, hops)))
                def _():
                    piece(c, BODY).start()

        if c > 0:
            @pl.when(plain)
            def _():
                piece(c, BODY).start()

    @pl.loop(EARLY, chunks)
    def _(c):
        kv_load(0, c).start()
        kv_load(1, c).start()

    @pl.when(has_left)
    def _():
        rim_copy().wait_recv()

    if line:
        @pl.when(guest)
        def _():
            guest_copy().wait_recv()
            pass_copy().start()

    @pl.when(jnp.logical_not(has_left))
    def _():
        rim_in[...] = jnp.zeros_like(rim_in)

        @pl.loop(0, chunks)
        def _(c):
            prev[c] = jnp.zeros((rows, width), jnp.bfloat16)

    for c in range(EARLY):
        for t in range(tiles):
            put_head(c, t, gate(c, t, 0, 16, *kv_rims(c, t)))

        @pl.when(has_right)
        def _():
            piece(c, HEAD).start()

    par_copy(1).start()

    @pl.loop(0, chunks)
    def _(c):
        q_load(c).start()

    loaded(kv.at[pl.ds(2 * EARLY, 2 * (chunks - EARLY))], 2)
    par_copy(2).start()

    @pl.loop(EARLY, chunks)
    def _(c):
        for t in range(tiles):
            block = gate(c, t, 0, rows, *kv_rims(c, t))
            put_head(c, t, block[:16])
            gated[c, BODY, pl.ds(t * LANES, LANES)] = block[16:]

        @pl.when(has_right)
        def _():
            piece(c).start()

    par_copy(1).wait()
    par_copy(2).wait()
    taps = lax.broadcasted_iota(jnp.int32, (FILT, 2 * LANES), 0)
    place = lax.broadcasted_iota(jnp.int32, (FILT, 2 * LANES), 1)
    total = taps + place
    for b in range(SUB):
        onehot = jnp.where(total == FILT + b, 1.0, 0.0).astype(jnp.bfloat16)
        moved = jnp.dot(filt[...], onehot, preferred_element_type=jnp.float32)
        for r in range(2):
            toep[r, pl.ds(b, groups, stride=SUB), :] = moved[:, r * LANES:(r + 1) * LANES]

    def operand(c, t):
        first = pl.multiple_of((c * tiles + t) * LANES, LANES)
        left_part = toep[0, pl.ds(first, LANES), :].astype(jnp.bfloat16)
        right_part = toep[1, pl.ds(first, LANES), :].astype(jnp.bfloat16)
        return left_part, right_part

    def factors(c, t, mine, rim):
        cols, lanes = columns(c, t), pl.ds(t * LANES, LANES)
        q_feat = featurize(q[c, :, lanes], rim, taps_of(0, cols))
        return q_feat, skip[:, cols] * mine.astype(jnp.float32)

    def mix(c):
        for t in range(tiles):
            lanes = pl.ds(t * LANES, LANES)
            mine = own(c, t)
            window = jnp.concatenate([prev[c, :, lanes], mine], axis=0)
            left_part, right_part = operand(c, t)
            lhs = jnp.concatenate([left_part, right_part[:, :SUB]], axis=1)
            conv = convolve(lhs, window)
            q_feat, direct = factors(c, t, mine, q_rim(c, t))
            mixed[c, :, lanes] = (q_feat * (conv + direct)).astype(jnp.bfloat16)

    loaded(q, 0)
    for b in range(1, hops + 1):
        carry(b)

    def stage(first, count, group):
        @pl.when(has_left)
        def _():
            arrived(first, count, group)

        @pl.loop(first, first + count)
        def _(c):
            mix(c)

    @pl.loop(0, quads)
    def _(i):
        stage(4 * i, 4, 1 + i)

    if spare:
        stage(4 * quads, spare, 1 + quads)
    stage(last - 1, 1, near)

    first = columns(last, 0).start
    end_taps[pl.ds(0, 2), :] = feat[0, pl.ds(1, 2), pl.ds(first, width)]
    for t in range(tiles):
        lanes = pl.ds(t * LANES, LANES)
        left_part, right_part = operand(last, t)
        end_lhs[t, :, :LANES] = left_part
        end_lhs[t, :, LANES:] = right_part
        mine = own(last, t)
        end_q[:, lanes], end_direct[:, lanes] = factors(last, t, mine, q_rim(last, t, True))
        end_window[pl.ds(rows, rows), lanes] = mine

    @pl.when(has_left)
    def _():
        arrived(last, 1, near + 1)

    end_window[pl.ds(0, rows), :] = prev[last]

    @pl.when(has_right)
    def _():
        rim_copy().wait_send()

    if line:
        @pl.when(guest)
        def _():
            pass_copy().wait_send()

    @pl.when(plain)
    def _():
        sent(gated, 0)

    def mostly(b):
        lost = 3 * width // 4 if b == 1 else b * width
        count = (chunks * rows * width - (rows - 16) * lost) // (2 * LANES)
        sent(toep.at[0, pl.ds(0, count)], 0)

    for b in range(1, hops + 1):
        @pl.when(jnp.logical_and(turns, behind == b))
        def _():
            mostly(b - 1)

        @pl.when(jnp.logical_and(carries, held(b)))
        def _():
            sent(hop.at[pl.ds(0, b), BODY], 2)

    if hops:
        @pl.when(jnp.logical_and(turns, behind > hops))
        def _():
            mostly(hops)


def drain(mixed, window, lhs, q_feat, direct, taps, out_hbm, ending, sem):
    chunks, _, width = mixed.shape
    last = chunks - 1
    row = lax.broadcasted_iota(jnp.int32, (16, LANES), 0)

    def lanes_of(t, base=0):
        return slice(base + t * LANES, base + (t + 1) * LANES)

    for c in range(last):
        pltpu.make_async_copy(
            mixed.at[c], out_hbm.at[:, c * width:(c + 1) * width], sem.at[0]).start()
    for t in range(width // LANES):
        lanes = lanes_of(t)
        conv = convolve(lhs[t, :, :FILT + SUB], window[:, lanes])
        more = jnp.where(
            row == 0, taps[:1, lanes], jnp.where(row == 1, taps[1:2, lanes], 0.0))
        more = more * window[:16, lanes].astype(jnp.float32)[:1]
        scale = jnp.concatenate([q_feat[:16, lanes] + more, q_feat[16:, lanes]], axis=0)
        ending[:, lanes] = (scale * (conv + direct[:, lanes])).astype(jnp.bfloat16)
        pltpu.make_async_copy(
            ending.at[:, lanes], out_hbm.at[:, lanes_of(t, last * width)], sem.at[0]).start()
    pltpu.make_async_copy(mixed, mixed, sem.at[0]).wait()


def shards(n, line, q_stream, k_stream, v_stream, feat_filter, long_filter, skip_gain):
    rows, channels = q_stream.shape
    groups = long_filter.shape[0]
    chunks = channels // CHUNK
    cut = pltpu.VMEM((chunks, rows, CHUNK), jnp.bfloat16)
    rim = pltpu.VMEM((8, channels // 2 + channels // 8), jnp.bfloat16)
    dma = pltpu.SemaphoreType.DMA
    hops = HOPS if line else 0
    arrivals = 5 + (chunks + 1) // 4
    hops = max(hops, 1)
    tiles = CHUNK // LANES
    parts = pl.pallas_call(
        functools.partial(kernel, n, line),
        out_shape=(
            cut, pltpu.VMEM((2 * rows, CHUNK), jnp.bfloat16),
            pltpu.VMEM((tiles, LANES, 2 * LANES), jnp.bfloat16),
            pltpu.VMEM((rows, CHUNK), jnp.float32), pltpu.VMEM((rows, CHUNK), jnp.float32),
            pltpu.VMEM((8, CHUNK), jnp.float32)),
        in_specs=[pl.BlockSpec(memory_space=pltpu.HBM)] * 6,
        out_specs=[pl.BlockSpec(memory_space=pltpu.VMEM)] * 6,
        scratch_shapes=[
            cut, pltpu.VMEM((2 * chunks, rows, CHUNK), jnp.bfloat16),
            pltpu.VMEM(feat_filter.shape, jnp.float32),
            pltpu.VMEM(long_filter.shape, jnp.bfloat16),
            pltpu.VMEM((1, channels), jnp.float32),
            pltpu.VMEM((3, 8, channels), jnp.bfloat16),
            rim, rim, rim,
            pltpu.VMEM((1, channels), jnp.float32),
            cut, cut,
            pltpu.VMEM((2, groups * SUB, LANES), jnp.float32),
            pltpu.VMEM((hops, rows, CHUNK), jnp.bfloat16),
            dma((3,)), dma((4,)), dma((arrivals,)),
            pltpu.SemaphoreType.REGULAR,
        ],
        compiler_params=pltpu.CompilerParams(
            collective_id=0, has_side_effects=True, vmem_limit_bytes=GRANT),
    )(q_stream, k_stream, v_stream, feat_filter, long_filter, skip_gain.reshape(1, channels))
    return pl.pallas_call(
        drain,
        out_shape=jax.ShapeDtypeStruct((rows, channels), jnp.bfloat16),
        in_specs=[pl.BlockSpec(memory_space=pltpu.VMEM)] * 6,
        out_specs=pl.BlockSpec(memory_space=pl.ANY),
        scratch_shapes=[pltpu.VMEM((rows, CHUNK), jnp.bfloat16), dma((1,))],
        compiler_params=pltpu.CompilerParams(vmem_limit_bytes=8 << 20),
    )(*parts)


def solution(mesh):
    n = mesh.shape["seq"]
    rows = P(("rep", "seq"), None)
    return jax.shard_map(
        functools.partial(shards, n, row_of(mesh)), mesh=mesh,
        in_specs=(rows, rows, rows, P(), P(), P()), out_specs=rows, check_vma=False)
```

```python
import functools

import jax
import jax.numpy as jnp
from jax import lax
from jax.experimental import pallas as pl
from jax.experimental.pallas import tpu as pltpu
from jax.sharding import PartitionSpec as P

GROUP_CH = 16
FILT = 128
FEAT = 3
LANES = 128
SUB = 16
CHUNK = 512
EARLY = 4
HOPS = 3
AHEAD = {2: (0, 96), 3: (2, 16)}
AIDE = 0
GRANT = 59 << 20
MESH = pl.DeviceIdType.MESH


def shifted(rim, x):
    ext = jnp.concatenate([rim, x], axis=0)
    return pltpu.roll(ext, 1, 0)[8:], pltpu.roll(ext, 2, 0)[8:]


def featurize(x, rim, taps):
    x = x.astype(jnp.float32)
    one, two = shifted(rim, x)
    return taps[0] * x + taps[1] * one + taps[2] * two


def row_of(mesh):
    ring = mesh.devices.reshape(-1, mesh.shape["seq"])[0]
    at = [getattr(d, "coords", None) for d in ring]
    if None in at:
        return 0
    apart = [sum(p != q for p, q in zip(a, b)) for a, b in zip(at, at[1:])]
    turns = [i + 1 for i, axes in enumerate(apart) if axes > 1]
    row = turns[0] if turns else 0
    return row if row > 2 and len(ring) % row == 0 else 0


def convolve(lhs, window):
    rows = window.shape[0] - FILT
    blocks = rows // SUB
    depth = FILT + SUB
    lane_group = lax.broadcasted_iota(jnp.int32, (SUB, LANES), 1) // GROUP_CH
    rhs = jnp.concatenate([window[a * SUB:a * SUB + depth] for a in range(blocks)], axis=1)
    every = jnp.dot(lhs, rhs, preferred_element_type=jnp.float32)
    conv = []
    for a in range(blocks):
        mine = every[:SUB, a * LANES:(a + 1) * LANES]
        for g in range(1, LANES // GROUP_CH):
            mine = jnp.where(
                lane_group == g,
                every[g * SUB:(g + 1) * SUB, a * LANES:(a + 1) * LANES], mine)
        conv.append(mine)
    return jnp.concatenate(conv, axis=0)


def kernel(
    n, line, q_hbm, k_hbm, v_hbm, feat_hbm, long_hbm, skip_hbm,
    mixed, end_window, end_lhs, end_q, end_direct, end_taps,
    q, kv, feat, filt, skip, ends, rim_out, rim_in, guest_in, tops, gated, prev, toep,
    hop, in_sem, send_sem, recv_sem, go,
):
    chunks, rows, width = gated.shape
    tiles = width // LANES
    groups = filt.shape[0]
    channels = chunks * width
    me = lax.axis_index("seq")
    right, left = lax.rem(me + 1, n), lax.rem(me + n - 1, n)
    has_left, has_right = me > 0, me < n - 1

    barrier = pltpu.get_barrier_semaphore()

    def greet(device):
        pl.semaphore_signal(barrier, inc=1, device_id={"seq": device}, device_id_type=MESH)

    if line:
        spot = lax.rem(me, line)
        host = jnp.logical_and(lax.rem(spot, 2) == 0, spot > 1)
        guest = jnp.logical_and(lax.rem(spot, 2) == 1, spot > 1)
        caller = jnp.logical_and(lax.rem(spot, 2) == 1, spot < line - 1)

        @pl.when(jnp.logical_and(has_left, jnp.logical_not(host)))
        def _():
            greet(left)

        @pl.when(caller)
        def _():
            greet(right)

        @pl.when(guest)
        def _():
            greet(jnp.maximum(me - 2, 0))

        @pl.when(host)
        def _():
            pl.semaphore_wait(barrier, 2)
            pl.semaphore_signal(go, inc=1, device_id={"seq": left}, device_id_type=MESH)
    else:
        @pl.when(has_left)
        def _():
            greet(left)

    hops = hop.shape[0] if line else 0
    half = channels // 2
    if line:
        level = me // line
        behind = n // line - 1 - level
        turns = jnp.logical_and(spot == line - 1, has_right)
        carries = jnp.logical_and(spot == AIDE, behind > 0)
        plain = jnp.logical_and(has_right, jnp.logical_not(turns))

        @pl.when(carries)
        def _():
            greet(jnp.minimum(me + line - 1 - AIDE, n - 1))
    else:
        plain = has_right

    streams = (k_hbm, v_hbm, q_hbm)

    def end_copy(i):
        return pltpu.make_async_copy(
            streams[i].at[pl.ds(rows - 8, 8)], ends.at[i], in_sem.at[0])

    def cols_of(c):
        return pl.ds(pl.multiple_of(c * width, width), width)

    def kv_load(i, c):
        return pltpu.make_async_copy(
            streams[i].at[:, cols_of(c)], kv.at[2 * c + i], in_sem.at[2])

    def loaded(part, slot):
        pltpu.make_async_copy(part, part, in_sem.at[slot]).wait()

    def q_load(c):
        return pltpu.make_async_copy(q_hbm.at[:, cols_of(c)], q.at[c], in_sem.at[0])

    params = ((feat_hbm, feat, 1), (long_hbm, filt, 1), (skip_hbm, skip, 2))

    def par_copy(i):
        src, dst, slot = params[i]
        return pltpu.make_async_copy(src, dst, in_sem.at[slot])

    for i in range(3):
        end_copy(i).start()
    par_copy(0).start()
    for c in range(EARLY):
        kv_load(0, c).start()
        kv_load(1, c).start()

    def remote(src, dst, send, recv, to=right):
        return pltpu.make_async_remote_copy(
            src_ref=src, dst_ref=dst, send_sem=send_sem.at[send], recv_sem=recv,
            device_id={"seq": to}, device_id_type=MESH)

    def rim_copy():
        return remote(rim_out, rim_in, 1, recv_sem.at[0])

    last = chunks - 1
    quads, spare = (last - 1) // 4, (last - 1) % 4
    near = 1 + quads + (1 if spare else 0)
    hop_slot = near + 2
    guest_slot = near + 3

    def slot(c):
        return jnp.where(c == last, near + 1, jnp.where(c == last - 1, near, 1 + c // 4))

    def guest_copy():
        return remote(
            rim_out, guest_in, 1, recv_sem.at[guest_slot], jnp.minimum(me + 2, n - 1))

    def pass_copy():
        return remote(guest_in, rim_in, 3, recv_sem.at[0], left)

    def piece(c, part=slice(None), lanes=slice(None)):
        return remote(
            gated.at[c, part, lanes], prev.at[c, part, lanes], 0, recv_sem.at[slot(c)])

    def sent(part, slot):
        pltpu.make_async_copy(part, part, send_sem.at[slot]).wait()

    def arrived(first, count, group):
        part = prev.at[pl.ds(first, count)]
        pltpu.make_async_copy(part, part, recv_sem.at[group]).wait()

    HEAD, BODY = pl.ds(0, 16), pl.ds(16, rows - 16)

    def hop_copy(h, part=BODY, send=None):
        if send is None:
            send = jnp.where(h == behind - 1, 0, 2)
        return remote(
            gated.at[h, part], hop.at[h, part], send, recv_sem.at[hop_slot],
            jnp.maximum(me - line + 1 + AIDE, 0))

    def lost(b):
        full, more = AHEAD.get(b, (b - 1, 0))
        return (full * (rows - 16) + more) * width // (2 * LANES)

    def forward_copy(h):
        return remote(
            hop.at[h, BODY], prev.at[h, BODY], 2, recv_sem.at[slot(h)],
            jnp.minimum(me + line - AIDE, n - 1))

    def held(b):
        return behind == b if b < hops else behind >= b

    def carry(b):
        @pl.when(jnp.logical_and(carries, held(b)))
        def _():
            part = hop.at[pl.ds(0, b), BODY]
            pltpu.make_async_copy(part, part, recv_sem.at[hop_slot]).wait()
            for h in range(b):
                forward_copy(h).start()

    row = lax.broadcasted_iota(jnp.int32, (8, LANES), 0)

    def last_rows(i, at):
        return ends[i, :, pl.ds(pl.multiple_of(at, LANES), LANES)].astype(jnp.float32)

    def pack_kv():
        @pl.loop(0, half // width)
        def _(c):
            for t in range(tiles):
                at = c * width + t * LANES
                packed = jnp.where(
                    row < 2, pltpu.roll(last_rows(0, at), 2, 0),
                    jnp.where(
                        row < 4, pltpu.roll(last_rows(1, at), 4, 0),
                        jnp.where(
                            row < 6, pltpu.roll(last_rows(0, at + half), 6, 0),
                            last_rows(1, at + half))))
                rim_out[:, pl.ds(pl.multiple_of(at, LANES), LANES)] = packed.astype(jnp.bfloat16)

    def pack_q():
        eighth = channels // 8

        @pl.loop(0, eighth // width)
        def _(c):
            for t in range(tiles):
                at = c * width + t * LANES
                packed = last_rows(2, at + 6 * eighth)
                for m in range(8):
                    if m != 6:
                        moved = pltpu.roll(last_rows(2, at + m * eighth), (m + 2) % 8, 0)
                        packed = jnp.where(row == m, moved, packed)
                rim_out[:, pl.ds(pl.multiple_of(half + at, LANES), LANES)] = packed.astype(
                    jnp.bfloat16)

    def taps_of(i, cols):
        return [feat[i, pl.ds(j, 1), cols] for j in range(FEAT)]

    def kv_rims(c, t):
        per_half = chunks // 2
        upper = c >= per_half
        at = lax.rem(c, per_half) * width + t * LANES
        x = rim_in[:, pl.ds(pl.multiple_of(at, LANES), LANES)].astype(jnp.float32)
        return (jnp.where(upper, pltpu.roll(x, 2, 0), pltpu.roll(x, 6, 0)),
                jnp.where(upper, x, pltpu.roll(x, 4, 0)))

    def q_rim(c, t, final=False):
        per_eighth = chunks // 8
        at = half + lax.rem(c, per_eighth) * width + t * LANES
        x = rim_in[:, pl.ds(pl.multiple_of(at, LANES), LANES)].astype(jnp.float32)
        two = jnp.sum(jnp.where(row == c // per_eighth, x, 0.0), axis=0, keepdims=True)
        rim = jnp.where(row == 6, two, 0.0)
        if final:
            return rim
        one = prev[c, HEAD, pl.ds(t * LANES, LANES)].astype(jnp.float32)[:1]
        return jnp.where(row == 7, one, rim)

    def columns(c, t):
        return pl.ds(pl.multiple_of(c * width + t * LANES, LANES), LANES)

    def gate(c, t, first, count, k_rim, v_rim):
        cols = columns(c, t)
        part, lanes = pl.ds(first, count), pl.ds(t * LANES, LANES)
        k_feat = featurize(kv[2 * c, part, lanes], k_rim, taps_of(1, cols))
        v_feat = featurize(kv[2 * c + 1, part, lanes], v_rim, taps_of(2, cols))
        return (k_feat * v_feat).astype(jnp.bfloat16)

    row16 = lax.broadcasted_iota(jnp.int32, (16, LANES), 0)

    def put_head(c, t, block):
        at = c * width + t * LANES
        tops[:, columns(c, t)] = block[:1].astype(jnp.float32)
        gated[c, HEAD, pl.ds(t * LANES, LANES)] = jnp.where(
            row16 == 0, last_rows(2, at)[7:], block.astype(jnp.float32)).astype(jnp.bfloat16)

    def own(c, t):
        lanes = pl.ds(t * LANES, LANES)
        head = jnp.where(
            row16 == 0, tops[:, columns(c, t)], gated[c, HEAD, lanes].astype(jnp.float32))
        return jnp.concatenate([head.astype(jnp.bfloat16), gated[c, BODY, lanes]], axis=0)

    loaded(ends, 0)
    pack_kv()
    pack_q()

    if line:
        @pl.when(turns)
        def _():
            pl.semaphore_wait(barrier, 2)

        @pl.when(caller)
        def _():
            pl.semaphore_wait(barrier, 1)
            guest_copy().start()

        alone = jnp.logical_or(jnp.logical_or(turns, host), caller)

        @pl.when(jnp.logical_and(has_right, jnp.logical_not(alone)))
        def _():
            pl.semaphore_wait(barrier, 1)

        near_by = jnp.logical_and(has_right, jnp.logical_not(caller))
    else:
        near_by = has_right

        @pl.when(has_right)
        def _():
            pl.semaphore_wait(barrier, 1)

    @pl.when(near_by)
    def _():
        rim_copy().start()

    zeros = jnp.zeros((8, LANES), jnp.float32)
    par_copy(0).wait()
    loaded(kv.at[pl.ds(0, 2 * EARLY)], 2)
    for c in range(EARLY):
        for t in range(tiles):
            lanes = pl.ds(t * LANES, LANES)
            gated[c, BODY, lanes] = gate(c, t, 0, rows, zeros, zeros)[16:]
            if line and c == 0 and t == 1:
                @pl.when(caller)
                def _():
                    pl.semaphore_wait(go, 1)

            if c == 0 and t % 2 == 1:
                @pl.when(plain)
                def _():
                    piece(0, BODY, pl.ds((t - 1) * LANES, 2 * LANES)).start()

        if hops:
            if c < hops:
                split = [(b, more) for b, (full, more) in AHEAD.items() if full == c]
                whole = jnp.logical_and(turns, c < behind)
                for b, more in split:
                    whole = jnp.logical_and(whole, behind != b)

                    @pl.when(jnp.logical_and(turns, behind == b))
                    def _():
                        hop_copy(c, pl.ds(16, more), 2).start()
                        hop_copy(c, pl.ds(16 + more, rows - 16 - more), 0).start()

                @pl.when(whole)
                def _():
                    hop_copy(c).start()

            if 1 < c <= hops:
                @pl.when(jnp.logical_and(turns, behind == c))
                def _():
                    sent(toep.at[0, pl.ds(0, lost(c))], 2)

            if c == hops:
                @pl.when(jnp.logical_and(turns, behind > c))
                def _():
                    sent(gated.at[pl.ds(0, c), BODY], 2)

            if c > 0:
                @pl.when(jnp.logical_and(turns, c >= jnp.minimum(behind, hops)))
                def _():
                    piece(c, BODY).start()

        if c > 0:
            @pl.when(plain)
            def _():
                piece(c, BODY).start()

    @pl.loop(EARLY, chunks)
    def _(c):
        kv_load(0, c).start()
        kv_load(1, c).start()

    @pl.when(has_left)
    def _():
        rim_copy().wait_recv()

    if line:
        @pl.when(guest)
        def _():
            guest_copy().wait_recv()
            pass_copy().start()

    @pl.when(jnp.logical_not(has_left))
    def _():
        rim_in[...] = jnp.zeros_like(rim_in)

        @pl.loop(0, chunks)
        def _(c):
            prev[c] = jnp.zeros((rows, width), jnp.bfloat16)

    for c in range(EARLY):
        for t in range(tiles):
            put_head(c, t, gate(c, t, 0, 16, *kv_rims(c, t)))

        @pl.when(has_right)
        def _():
            piece(c, HEAD).start()

    par_copy(1).start()

    @pl.loop(0, chunks)
    def _(c):
        q_load(c).start()

    loaded(kv.at[pl.ds(2 * EARLY, 2 * (chunks - EARLY))], 2)
    par_copy(2).start()

    @pl.loop(EARLY, chunks)
    def _(c):
        for t in range(tiles):
            block = gate(c, t, 0, rows, *kv_rims(c, t))
            put_head(c, t, block[:16])
            gated[c, BODY, pl.ds(t * LANES, LANES)] = block[16:]

        @pl.when(has_right)
        def _():
            piece(c).start()

    par_copy(1).wait()
    par_copy(2).wait()
    taps = lax.broadcasted_iota(jnp.int32, (FILT, 2 * LANES), 0)
    place = lax.broadcasted_iota(jnp.int32, (FILT, 2 * LANES), 1)
    total = taps + place
    for b in range(SUB):
        onehot = jnp.where(total == FILT + b, 1.0, 0.0).astype(jnp.bfloat16)
        moved = jnp.dot(filt[...], onehot, preferred_element_type=jnp.float32)
        for r in range(2):
            toep[r, pl.ds(b, groups, stride=SUB), :] = moved[:, r * LANES:(r + 1) * LANES]

    def operand(c, t):
        first = pl.multiple_of((c * tiles + t) * LANES, LANES)
        left_part = toep[0, pl.ds(first, LANES), :].astype(jnp.bfloat16)
        right_part = toep[1, pl.ds(first, LANES), :].astype(jnp.bfloat16)
        return left_part, right_part

    def factors(c, t, mine, rim):
        cols, lanes = columns(c, t), pl.ds(t * LANES, LANES)
        q_feat = featurize(q[c, :, lanes], rim, taps_of(0, cols))
        return q_feat, skip[:, cols] * mine.astype(jnp.float32)

    def mix(c):
        for t in range(tiles):
            lanes = pl.ds(t * LANES, LANES)
            mine = own(c, t)
            window = jnp.concatenate([prev[c, :, lanes], mine], axis=0)
            left_part, right_part = operand(c, t)
            lhs = jnp.concatenate([left_part, right_part[:, :SUB]], axis=1)
            conv = convolve(lhs, window)
            q_feat, direct = factors(c, t, mine, q_rim(c, t))
            mixed[c, :, lanes] = (q_feat * (conv + direct)).astype(jnp.bfloat16)

    loaded(q, 0)
    for b in range(1, hops + 1):
        carry(b)

    def stage(first, count, group):
        @pl.when(has_left)
        def _():
            arrived(first, count, group)

        @pl.loop(first, first + count)
        def _(c):
            mix(c)

    @pl.loop(0, quads)
    def _(i):
        stage(4 * i, 4, 1 + i)

    if spare:
        stage(4 * quads, spare, 1 + quads)
    stage(last - 1, 1, near)

    first = columns(last, 0).start
    end_taps[pl.ds(0, 2), :] = feat[0, pl.ds(1, 2), pl.ds(first, width)]
    for t in range(tiles):
        lanes = pl.ds(t * LANES, LANES)
        left_part, right_part = operand(last, t)
        end_lhs[t, :, :LANES] = left_part
        end_lhs[t, :, LANES:] = right_part
        mine = own(last, t)
        end_q[:, lanes], end_direct[:, lanes] = factors(last, t, mine, q_rim(last, t, True))
        end_window[pl.ds(rows, rows), lanes] = mine

    @pl.when(has_left)
    def _():
        arrived(last, 1, near + 1)

    end_window[pl.ds(0, rows), :] = prev[last]

    @pl.when(has_right)
    def _():
        rim_copy().wait_send()

    if line:
        @pl.when(guest)
        def _():
            pass_copy().wait_send()

    @pl.when(plain)
    def _():
        sent(gated, 0)

    def mostly(b):
        count = chunks * rows * width // (2 * LANES) - lost(b + 1)
        sent(toep.at[0, pl.ds(0, count)], 0)

    for b in range(1, hops + 1):
        @pl.when(jnp.logical_and(turns, behind == b))
        def _():
            mostly(b - 1)

        @pl.when(jnp.logical_and(carries, held(b)))
        def _():
            sent(hop.at[pl.ds(0, b), BODY], 2)

    if hops:
        @pl.when(jnp.logical_and(turns, behind > hops))
        def _():
            mostly(hops)


def drain(mixed, window, lhs, q_feat, direct, taps, out_hbm, ending, sem):
    chunks, _, width = mixed.shape
    last = chunks - 1
    row = lax.broadcasted_iota(jnp.int32, (16, LANES), 0)

    def lanes_of(t, base=0):
        return slice(base + t * LANES, base + (t + 1) * LANES)

    for c in range(last):
        pltpu.make_async_copy(
            mixed.at[c], out_hbm.at[:, c * width:(c + 1) * width], sem.at[0]).start()
    for t in range(width // LANES):
        lanes = lanes_of(t)
        conv = convolve(lhs[t, :, :FILT + SUB], window[:, lanes])
        more = jnp.where(
            row == 0, taps[:1, lanes], jnp.where(row == 1, taps[1:2, lanes], 0.0))
        more = more * window[:16, lanes].astype(jnp.float32)[:1]
        scale = jnp.concatenate([q_feat[:16, lanes] + more, q_feat[16:, lanes]], axis=0)
        ending[:, lanes] = (scale * (conv + direct[:, lanes])).astype(jnp.bfloat16)
        pltpu.make_async_copy(
            ending.at[:, lanes], out_hbm.at[:, lanes_of(t, last * width)], sem.at[0]).start()
    pltpu.make_async_copy(mixed, mixed, sem.at[0]).wait()


def shards(n, line, q_stream, k_stream, v_stream, feat_filter, long_filter, skip_gain):
    rows, channels = q_stream.shape
    groups = long_filter.shape[0]
    chunks = channels // CHUNK
    cut = pltpu.VMEM((chunks, rows, CHUNK), jnp.bfloat16)
    rim = pltpu.VMEM((8, channels // 2 + channels // 8), jnp.bfloat16)
    dma = pltpu.SemaphoreType.DMA
    hops = HOPS if line else 0
    arrivals = 5 + (chunks + 1) // 4
    hops = max(hops, 1)
    tiles = CHUNK // LANES
    parts = pl.pallas_call(
        functools.partial(kernel, n, line),
        out_shape=(
            cut, pltpu.VMEM((2 * rows, CHUNK), jnp.bfloat16),
            pltpu.VMEM((tiles, LANES, 2 * LANES), jnp.bfloat16),
            pltpu.VMEM((rows, CHUNK), jnp.float32), pltpu.VMEM((rows, CHUNK), jnp.float32),
            pltpu.VMEM((8, CHUNK), jnp.float32)),
        in_specs=[pl.BlockSpec(memory_space=pltpu.HBM)] * 6,
        out_specs=[pl.BlockSpec(memory_space=pltpu.VMEM)] * 6,
        scratch_shapes=[
            cut, pltpu.VMEM((2 * chunks, rows, CHUNK), jnp.bfloat16),
            pltpu.VMEM(feat_filter.shape, jnp.float32),
            pltpu.VMEM(long_filter.shape, jnp.bfloat16),
            pltpu.VMEM((1, channels), jnp.float32),
            pltpu.VMEM((3, 8, channels), jnp.bfloat16),
            rim, rim, rim,
            pltpu.VMEM((1, channels), jnp.float32),
            cut, cut,
            pltpu.VMEM((2, groups * SUB, LANES), jnp.float32),
            pltpu.VMEM((hops, rows, CHUNK), jnp.bfloat16),
            dma((3,)), dma((4,)), dma((arrivals,)),
            pltpu.SemaphoreType.REGULAR,
        ],
        compiler_params=pltpu.CompilerParams(
            collective_id=0, has_side_effects=True, vmem_limit_bytes=GRANT),
    )(q_stream, k_stream, v_stream, feat_filter, long_filter, skip_gain.reshape(1, channels))
    return pl.pallas_call(
        drain,
        out_shape=jax.ShapeDtypeStruct((rows, channels), jnp.bfloat16),
        in_specs=[pl.BlockSpec(memory_space=pltpu.VMEM)] * 6,
        out_specs=pl.BlockSpec(memory_space=pl.ANY),
        scratch_shapes=[pltpu.VMEM((rows, CHUNK), jnp.bfloat16), dma((1,))],
        compiler_params=pltpu.CompilerParams(vmem_limit_bytes=8 << 20),
    )(*parts)


def solution(mesh):
    n = mesh.shape["seq"]
    rows = P(("rep", "seq"), None)
    return jax.shard_map(
        functools.partial(shards, n, row_of(mesh)), mesh=mesh,
        in_specs=(rows, rows, rows, P(), P(), P()), out_specs=rows, check_vma=False)
```

```python
import functools

import jax
import jax.numpy as jnp
from jax import lax
from jax.experimental import pallas as pl
from jax.experimental.pallas import tpu as pltpu
from jax.sharding import PartitionSpec as P

GROUP_CH = 16
FILT = 128
FEAT = 3
LANES = 128
SUB = 16
CHUNK = 512
EARLY = 4
HOPS = 3
AIDE = 0
GRANT = 59 << 20
MESH = pl.DeviceIdType.MESH


def shifted(rim, x):
    ext = jnp.concatenate([rim, x], axis=0)
    return pltpu.roll(ext, 1, 0)[8:], pltpu.roll(ext, 2, 0)[8:]


def featurize(x, rim, taps):
    x = x.astype(jnp.float32)
    one, two = shifted(rim, x)
    return taps[0] * x + taps[1] * one + taps[2] * two


def row_of(mesh):
    ring = mesh.devices.reshape(-1, mesh.shape["seq"])[0]
    at = [getattr(d, "coords", None) for d in ring]
    if None in at:
        return 0
    apart = [sum(p != q for p, q in zip(a, b)) for a, b in zip(at, at[1:])]
    turns = [i + 1 for i, axes in enumerate(apart) if axes > 1]
    row = turns[0] if turns else 0
    return row if row > 2 and len(ring) % row == 0 else 0


def convolve(lhs, window):
    rows = window.shape[0] - FILT
    blocks = rows // SUB
    depth = FILT + SUB
    lane_group = lax.broadcasted_iota(jnp.int32, (SUB, LANES), 1) // GROUP_CH
    rhs = jnp.concatenate([window[a * SUB:a * SUB + depth] for a in range(blocks)], axis=1)
    every = jnp.dot(lhs, rhs, preferred_element_type=jnp.float32)
    conv = []
    for a in range(blocks):
        mine = every[:SUB, a * LANES:(a + 1) * LANES]
        for g in range(1, LANES // GROUP_CH):
            mine = jnp.where(
                lane_group == g,
                every[g * SUB:(g + 1) * SUB, a * LANES:(a + 1) * LANES], mine)
        conv.append(mine)
    return jnp.concatenate(conv, axis=0)


def kernel(
    n, line, q_hbm, k_hbm, v_hbm, feat_hbm, long_hbm, skip_hbm,
    mixed, end_window, end_lhs, end_q, end_direct, end_taps,
    q, kv, feat, filt, skip, ends, rim_out, rim_in, guest_in, tops, gated, prev, toep,
    hop, in_sem, send_sem, recv_sem, go,
):
    chunks, rows, width = gated.shape
    tiles = width // LANES
    groups = filt.shape[0]
    channels = chunks * width
    me = lax.axis_index("seq")
    right, left = lax.rem(me + 1, n), lax.rem(me + n - 1, n)
    has_left, has_right = me > 0, me < n - 1

    barrier = pltpu.get_barrier_semaphore()

    def greet(device):
        pl.semaphore_signal(barrier, inc=1, device_id={"seq": device}, device_id_type=MESH)

    if line:
        spot = lax.rem(me, line)
        host = jnp.logical_and(lax.rem(spot, 2) == 0, spot > 1)
        guest = jnp.logical_and(lax.rem(spot, 2) == 1, spot > 1)
        caller = jnp.logical_and(lax.rem(spot, 2) == 1, spot < line - 1)

        @pl.when(caller)
        def _():
            greet(right)

        @pl.when(guest)
        def _():
            greet(jnp.maximum(me - 2, 0))

        @pl.when(jnp.logical_and(has_left, jnp.logical_not(host)))
        def _():
            greet(left)

        @pl.when(host)
        def _():
            pl.semaphore_wait(barrier, 2)
            pl.semaphore_signal(go, inc=1, device_id={"seq": left}, device_id_type=MESH)
    else:
        @pl.when(has_left)
        def _():
            greet(left)

    hops = hop.shape[0] if line else 0
    half = channels // 2
    if line:
        level = me // line
        behind = n // line - 1 - level
        turns = jnp.logical_and(spot == line - 1, has_right)
        carries = jnp.logical_and(spot == AIDE, behind > 0)
        plain = jnp.logical_and(has_right, jnp.logical_not(turns))

        @pl.when(carries)
        def _():
            greet(jnp.minimum(me + line - 1 - AIDE, n - 1))
    else:
        plain = has_right

    streams = (k_hbm, v_hbm, q_hbm)

    def end_copy(i):
        return pltpu.make_async_copy(
            streams[i].at[pl.ds(rows - 8, 8)], ends.at[i], in_sem.at[0])

    def cols_of(c):
        return pl.ds(pl.multiple_of(c * width, width), width)

    def kv_load(i, c):
        return pltpu.make_async_copy(
            streams[i].at[:, cols_of(c)], kv.at[2 * c + i], in_sem.at[2])

    def loaded(part, slot):
        pltpu.make_async_copy(part, part, in_sem.at[slot]).wait()

    def q_load(c):
        return pltpu.make_async_copy(q_hbm.at[:, cols_of(c)], q.at[c], in_sem.at[0])

    params = ((feat_hbm, feat, 1), (long_hbm, filt, 1), (skip_hbm, skip, 2))

    def par_copy(i):
        src, dst, slot = params[i]
        return pltpu.make_async_copy(src, dst, in_sem.at[slot])

    for i in range(3):
        end_copy(i).start()
    par_copy(0).start()
    for c in range(EARLY):
        kv_load(0, c).start()
        kv_load(1, c).start()

    def remote(src, dst, send, recv, to=right):
        return pltpu.make_async_remote_copy(
            src_ref=src, dst_ref=dst, send_sem=send_sem.at[send], recv_sem=recv,
            device_id={"seq": to}, device_id_type=MESH)

    def rim_copy():
        return remote(rim_out, rim_in, 1, recv_sem.at[0])

    last = chunks - 1
    quads, spare = (last - 1) // 4, (last - 1) % 4
    near = 1 + quads + (1 if spare else 0)
    hop_slot = near + 2
    guest_slot = hop_slot

    def slot(c):
        return jnp.where(c == last, near + 1, jnp.where(c == last - 1, near, 1 + c // 4))

    def guest_copy():
        return remote(
            rim_out, guest_in, 1, recv_sem.at[guest_slot], jnp.minimum(me + 2, n - 1))

    def pass_copy():
        return remote(guest_in, rim_in, 3, recv_sem.at[0], left)

    def piece(c, part=slice(None), lanes=slice(None)):
        return remote(
            gated.at[c, part, lanes], prev.at[c, part, lanes], 0, recv_sem.at[slot(c)])

    def sent(part, slot):
        pltpu.make_async_copy(part, part, send_sem.at[slot]).wait()

    def arrived(first, count, group):
        part = prev.at[pl.ds(first, count)]
        pltpu.make_async_copy(part, part, recv_sem.at[group]).wait()

    HEAD, BODY = pl.ds(0, 16), pl.ds(16, rows - 16)

    def hop_copy(h, lanes=slice(None), send=None):
        if send is None:
            send = jnp.where(h == behind - 1, 0, 2)
        return remote(
            gated.at[h, BODY, lanes], hop.at[h, BODY, lanes], send, recv_sem.at[hop_slot],
            jnp.maximum(me - line + 1 + AIDE, 0))

    SOON, LATE = pl.ds(0, 3 * width // 4), pl.ds(3 * width // 4, width // 4)

    def forward_copy(h):
        return remote(
            hop.at[h, BODY], prev.at[h, BODY], 2, recv_sem.at[slot(h)],
            jnp.minimum(me + line - AIDE, n - 1))

    def held(b):
        return behind == b if b < hops else behind >= b

    def carry(b):
        @pl.when(jnp.logical_and(carries, held(b)))
        def _():
            part = hop.at[pl.ds(0, b), BODY]
            pltpu.make_async_copy(part, part, recv_sem.at[hop_slot]).wait()
            for h in range(b):
                forward_copy(h).start()

    row = lax.broadcasted_iota(jnp.int32, (8, LANES), 0)

    def last_rows(i, at):
        return ends[i, :, pl.ds(pl.multiple_of(at, LANES), LANES)].astype(jnp.float32)

    def pack_kv():
        @pl.loop(0, half // width)
        def _(c):
            for t in range(tiles):
                at = c * width + t * LANES
                packed = jnp.where(
                    row < 2, pltpu.roll(last_rows(0, at), 2, 0),
                    jnp.where(
                        row < 4, pltpu.roll(last_rows(1, at), 4, 0),
                        jnp.where(
                            row < 6, pltpu.roll(last_rows(0, at + half), 6, 0),
                            last_rows(1, at + half))))
                rim_out[:, pl.ds(pl.multiple_of(at, LANES), LANES)] = packed.astype(jnp.bfloat16)

    def pack_q():
        eighth = channels // 8

        @pl.loop(0, eighth // width)
        def _(c):
            for t in range(tiles):
                at = c * width + t * LANES
                packed = last_rows(2, at + 6 * eighth)
                for m in range(8):
                    if m != 6:
                        moved = pltpu.roll(last_rows(2, at + m * eighth), (m + 2) % 8, 0)
                        packed = jnp.where(row == m, moved, packed)
                rim_out[:, pl.ds(pl.multiple_of(half + at, LANES), LANES)] = packed.astype(
                    jnp.bfloat16)

    def taps_of(i, cols):
        return [feat[i, pl.ds(j, 1), cols] for j in range(FEAT)]

    def kv_rims(c, t):
        per_half = chunks // 2
        upper = c >= per_half
        at = lax.rem(c, per_half) * width + t * LANES
        x = rim_in[:, pl.ds(pl.multiple_of(at, LANES), LANES)].astype(jnp.float32)
        return (jnp.where(upper, pltpu.roll(x, 2, 0), pltpu.roll(x, 6, 0)),
                jnp.where(upper, x, pltpu.roll(x, 4, 0)))

    def q_rim(c, t, final=False):
        per_eighth = chunks // 8
        at = half + lax.rem(c, per_eighth) * width + t * LANES
        x = rim_in[:, pl.ds(pl.multiple_of(at, LANES), LANES)].astype(jnp.float32)
        two = jnp.sum(jnp.where(row == c // per_eighth, x, 0.0), axis=0, keepdims=True)
        rim = jnp.where(row == 6, two, 0.0)
        if final:
            return rim
        one = prev[c, HEAD, pl.ds(t * LANES, LANES)].astype(jnp.float32)[:1]
        return jnp.where(row == 7, one, rim)

    def columns(c, t):
        return pl.ds(pl.multiple_of(c * width + t * LANES, LANES), LANES)

    def gate(c, t, first, count, k_rim, v_rim):
        cols = columns(c, t)
        part, lanes = pl.ds(first, count), pl.ds(t * LANES, LANES)
        k_feat = featurize(kv[2 * c, part, lanes], k_rim, taps_of(1, cols))
        v_feat = featurize(kv[2 * c + 1, part, lanes], v_rim, taps_of(2, cols))
        return (k_feat * v_feat).astype(jnp.bfloat16)

    row16 = lax.broadcasted_iota(jnp.int32, (16, LANES), 0)

    def put_head(c, t, block):
        at = c * width + t * LANES
        tops[:, columns(c, t)] = block[:1].astype(jnp.float32)
        gated[c, HEAD, pl.ds(t * LANES, LANES)] = jnp.where(
            row16 == 0, last_rows(2, at)[7:], block.astype(jnp.float32)).astype(jnp.bfloat16)

    def own(c, t):
        lanes = pl.ds(t * LANES, LANES)
        head = jnp.where(
            row16 == 0, tops[:, columns(c, t)], gated[c, HEAD, lanes].astype(jnp.float32))
        return jnp.concatenate([head.astype(jnp.bfloat16), gated[c, BODY, lanes]], axis=0)

    loaded(ends, 0)
    pack_kv()
    pack_q()

    if line:
        @pl.when(turns)
        def _():
            pl.semaphore_wait(barrier, 2)

        @pl.when(caller)
        def _():
            pl.semaphore_wait(barrier, 1)
            guest_copy().start()

        alone = jnp.logical_or(jnp.logical_or(turns, host), caller)

        @pl.when(jnp.logical_and(has_right, jnp.logical_not(alone)))
        def _():
            pl.semaphore_wait(barrier, 1)

        near_by = jnp.logical_and(has_right, jnp.logical_not(caller))
    else:
        near_by = has_right

        @pl.when(has_right)
        def _():
            pl.semaphore_wait(barrier, 1)

    @pl.when(near_by)
    def _():
        rim_copy().start()

    zeros = jnp.zeros((8, LANES), jnp.float32)
    par_copy(0).wait()
    loaded(kv.at[pl.ds(0, 2 * EARLY)], 2)
    for c in range(EARLY):
        for t in range(tiles):
            lanes = pl.ds(t * LANES, LANES)
            gated[c, BODY, lanes] = gate(c, t, 0, rows, zeros, zeros)[16:]
            if line and c == 0 and t == 1:
                @pl.when(caller)
                def _():
                    pl.semaphore_wait(go, 1)

            if c == 0 and t % 2 == 1:
                @pl.when(plain)
                def _():
                    piece(0, BODY, pl.ds((t - 1) * LANES, 2 * LANES)).start()

        if hops:
            if c < hops:
                halved = behind == 2 if c == 0 else False

                @pl.when(jnp.logical_and(
                    turns, jnp.logical_and(c < behind, jnp.logical_not(halved))))
                def _():
                    hop_copy(c).start()

                @pl.when(jnp.logical_and(turns, halved))
                def _():
                    hop_copy(c, SOON, 2).start()
                    hop_copy(c, LATE, 0).start()

            if 1 < c <= hops:
                @pl.when(jnp.logical_and(turns, behind == c))
                def _():
                    if c == 2:
                        sent(gated.at[0, BODY, SOON], 2)
                    else:
                        sent(gated.at[pl.ds(0, c - 1), BODY], 2)

            if c == hops:
                @pl.when(jnp.logical_and(turns, behind > c))
                def _():
                    sent(gated.at[pl.ds(0, c), BODY], 2)

            if c > 0:
                @pl.when(jnp.logical_and(turns, c >= jnp.minimum(behind, hops)))
                def _():
                    piece(c, BODY).start()

        if c > 0:
            @pl.when(plain)
            def _():
                piece(c, BODY).start()

    @pl.loop(EARLY, chunks)
    def _(c):
        kv_load(0, c).start()
        kv_load(1, c).start()

    @pl.when(has_left)
    def _():
        rim_copy().wait_recv()

    if line:
        @pl.when(guest)
        def _():
            guest_copy().wait_recv()
            pass_copy().start()

    @pl.when(jnp.logical_not(has_left))
    def _():
        rim_in[...] = jnp.zeros_like(rim_in)

        @pl.loop(0, chunks)
        def _(c):
            prev[c] = jnp.zeros((rows, width), jnp.bfloat16)

    for c in range(EARLY):
        for t in range(tiles):
            put_head(c, t, gate(c, t, 0, 16, *kv_rims(c, t)))

        @pl.when(has_right)
        def _():
            piece(c, HEAD).start()

    par_copy(1).start()

    @pl.loop(0, chunks)
    def _(c):
        q_load(c).start()

    loaded(kv.at[pl.ds(2 * EARLY, 2 * (chunks - EARLY))], 2)
    par_copy(2).start()

    @pl.loop(EARLY, chunks)
    def _(c):
        for t in range(tiles):
            block = gate(c, t, 0, rows, *kv_rims(c, t))
            put_head(c, t, block[:16])
            gated[c, BODY, pl.ds(t * LANES, LANES)] = block[16:]

        @pl.when(has_right)
        def _():
            piece(c).start()

    par_copy(1).wait()
    par_copy(2).wait()
    taps = lax.broadcasted_iota(jnp.int32, (FILT, 2 * LANES), 0)
    place = lax.broadcasted_iota(jnp.int32, (FILT, 2 * LANES), 1)
    total = taps + place
    for b in range(SUB):
        onehot = jnp.where(total == FILT + b, 1.0, 0.0).astype(jnp.bfloat16)
        moved = jnp.dot(filt[...], onehot, preferred_element_type=jnp.float32)
        for r in range(2):
            toep[r, pl.ds(b, groups, stride=SUB), :] = moved[:, r * LANES:(r + 1) * LANES]

    def operand(c, t):
        first = pl.multiple_of((c * tiles + t) * LANES, LANES)
        left_part = toep[0, pl.ds(first, LANES), :].astype(jnp.bfloat16)
        right_part = toep[1, pl.ds(first, LANES), :].astype(jnp.bfloat16)
        return left_part, right_part

    def factors(c, t, mine, rim):
        cols, lanes = columns(c, t), pl.ds(t * LANES, LANES)
        q_feat = featurize(q[c, :, lanes], rim, taps_of(0, cols))
        return q_feat, skip[:, cols] * mine.astype(jnp.float32)

    def mix(c):
        for t in range(tiles):
            lanes = pl.ds(t * LANES, LANES)
            mine = own(c, t)
            window = jnp.concatenate([prev[c, :, lanes], mine], axis=0)
            left_part, right_part = operand(c, t)
            lhs = jnp.concatenate([left_part, right_part[:, :SUB]], axis=1)
            conv = convolve(lhs, window)
            q_feat, direct = factors(c, t, mine, q_rim(c, t))
            mixed[c, :, lanes] = (q_feat * (conv + direct)).astype(jnp.bfloat16)

    loaded(q, 0)
    for b in range(1, hops + 1):
        carry(b)

    def stage(first, count, group):
        @pl.when(has_left)
        def _():
            arrived(first, count, group)

        @pl.loop(first, first + count)
        def _(c):
            mix(c)

    @pl.loop(0, quads)
    def _(i):
        stage(4 * i, 4, 1 + i)

    if spare:
        stage(4 * quads, spare, 1 + quads)
    stage(last - 1, 1, near)

    first = columns(last, 0).start
    end_taps[pl.ds(0, 2), :] = feat[0, pl.ds(1, 2), pl.ds(first, width)]
    for t in range(tiles):
        lanes = pl.ds(t * LANES, LANES)
        left_part, right_part = operand(last, t)
        end_lhs[t, :, :LANES] = left_part
        end_lhs[t, :, LANES:] = right_part
        mine = own(last, t)
        end_q[:, lanes], end_direct[:, lanes] = factors(last, t, mine, q_rim(last, t, True))
        end_window[pl.ds(rows, rows), lanes] = mine

    @pl.when(has_left)
    def _():
        arrived(last, 1, near + 1)

    end_window[pl.ds(0, rows), :] = prev[last]

    @pl.when(has_right)
    def _():
        rim_copy().wait_send()

    if line:
        @pl.when(guest)
        def _():
            pass_copy().wait_send()

    @pl.when(plain)
    def _():
        sent(gated, 0)

    def mostly(b):
        lost = 3 * width // 4 if b == 1 else b * width
        count = (chunks * rows * width - (rows - 16) * lost) // (2 * LANES)
        sent(toep.at[0, pl.ds(0, count)], 0)

    for b in range(1, hops + 1):
        @pl.when(jnp.logical_and(turns, behind == b))
        def _():
            mostly(b - 1)

        @pl.when(jnp.logical_and(carries, held(b)))
        def _():
            sent(hop.at[pl.ds(0, b), BODY], 2)

    if hops:
        @pl.when(jnp.logical_and(turns, behind > hops))
        def _():
            mostly(hops)


def drain(mixed, window, lhs, q_feat, direct, taps, out_hbm, ending, sem):
    chunks, _, width = mixed.shape
    last = chunks - 1
    row = lax.broadcasted_iota(jnp.int32, (16, LANES), 0)

    def lanes_of(t, base=0):
        return slice(base + t * LANES, base + (t + 1) * LANES)

    for c in range(last):
        pltpu.make_async_copy(
            mixed.at[c], out_hbm.at[:, c * width:(c + 1) * width], sem.at[0]).start()
    for t in range(width // LANES):
        lanes = lanes_of(t)
        conv = convolve(lhs[t, :, :FILT + SUB], window[:, lanes])
        more = jnp.where(
            row == 0, taps[:1, lanes], jnp.where(row == 1, taps[1:2, lanes], 0.0))
        more = more * window[:16, lanes].astype(jnp.float32)[:1]
        scale = jnp.concatenate([q_feat[:16, lanes] + more, q_feat[16:, lanes]], axis=0)
        ending[:, lanes] = (scale * (conv + direct[:, lanes])).astype(jnp.bfloat16)
        pltpu.make_async_copy(
            ending.at[:, lanes], out_hbm.at[:, lanes_of(t, last * width)], sem.at[0]).start()
    pltpu.make_async_copy(mixed, mixed, sem.at[0]).wait()


def shards(n, line, q_stream, k_stream, v_stream, feat_filter, long_filter, skip_gain):
    rows, channels = q_stream.shape
    groups = long_filter.shape[0]
    chunks = channels // CHUNK
    cut = pltpu.VMEM((chunks, rows, CHUNK), jnp.bfloat16)
    rim = pltpu.VMEM((8, channels // 2 + channels // 8), jnp.bfloat16)
    dma = pltpu.SemaphoreType.DMA
    hops = HOPS if line else 0
    arrivals = 4 + (chunks + 1) // 4
    hops = max(hops, 1)
    tiles = CHUNK // LANES
    parts = pl.pallas_call(
        functools.partial(kernel, n, line),
        out_shape=(
            cut, pltpu.VMEM((2 * rows, CHUNK), jnp.bfloat16),
            pltpu.VMEM((tiles, LANES, 2 * LANES), jnp.bfloat16),
            pltpu.VMEM((rows, CHUNK), jnp.float32), pltpu.VMEM((rows, CHUNK), jnp.float32),
            pltpu.VMEM((8, CHUNK), jnp.float32)),
        in_specs=[pl.BlockSpec(memory_space=pltpu.HBM)] * 6,
        out_specs=[pl.BlockSpec(memory_space=pltpu.VMEM)] * 6,
        scratch_shapes=[
            cut, pltpu.VMEM((2 * chunks, rows, CHUNK), jnp.bfloat16),
            pltpu.VMEM(feat_filter.shape, jnp.float32),
            pltpu.VMEM(long_filter.shape, jnp.bfloat16),
            pltpu.VMEM((1, channels), jnp.float32),
            pltpu.VMEM((3, 8, channels), jnp.bfloat16),
            rim, rim, rim,
            pltpu.VMEM((1, channels), jnp.float32),
            cut, cut,
            pltpu.VMEM((2, groups * SUB, LANES), jnp.float32),
            pltpu.VMEM((hops, rows, CHUNK), jnp.bfloat16),
            dma((3,)), dma((4,)), dma((arrivals,)),
            pltpu.SemaphoreType.REGULAR,
        ],
        compiler_params=pltpu.CompilerParams(
            collective_id=0, has_side_effects=True, vmem_limit_bytes=GRANT),
    )(q_stream, k_stream, v_stream, feat_filter, long_filter, skip_gain.reshape(1, channels))
    return pl.pallas_call(
        drain,
        out_shape=jax.ShapeDtypeStruct((rows, channels), jnp.bfloat16),
        in_specs=[pl.BlockSpec(memory_space=pltpu.VMEM)] * 6,
        out_specs=pl.BlockSpec(memory_space=pl.ANY),
        scratch_shapes=[pltpu.VMEM((rows, CHUNK), jnp.bfloat16), dma((1,))],
        compiler_params=pltpu.CompilerParams(vmem_limit_bytes=8 << 20),
    )(*parts)


def solution(mesh):
    n = mesh.shape["seq"]
    rows = P(("rep", "seq"), None)
    return jax.shard_map(
        functools.partial(shards, n, row_of(mesh)), mesh=mesh,
        in_specs=(rows, rows, rows, P(), P(), P()), out_specs=rows, check_vma=False)
```
